512 devices in a mesh: gx: 32 (over z, core), gy: 16 (over y, x).
Axes of the slice: x: 4, y: 4, z: 16, core: 2. Of those that a mesh axis runs over, the one named last changes fastest.
Arguments:
- start_field: float32 [16, 512, 4096], P(None, 'gx', 'gy'), may hold values from -6 to 6
- classes: int32 [512, 4096], P('gx', 'gy'), may hold values from 0 to 7
- conductor: int32 [512, 4096], P('gx', 'gy'), may hold values from 0 to 15
- drive: float32 [512, 4096], P('gx', 'gy'), may hold values from -6 to 6
- perm_table: float32 [8], replicated, may hold values from 1 to 4
- leaf_x: float32 [512, 4096], P('gx', 'gy'), may hold values from -1.5 to 1.5
- leaf_y: float32 [512, 4096], P('gx', 'gy'), may hold values from -1.5 to 1.5
- fwd_x: float32 [8192, 4096], P('gx', 'gy'), may hold values from -1 to 1
- back_x: float32 [8192, 4096], P('gx', 'gy'), may hold values from -1 to 1
- couple_x: float32 [8192, 4096], P('gx', 'gy'), may hold values from -0.375 to 0.375
- fwd_y: float32 [8192, 4096], P('gx', 'gy'), may hold values from -1 to 1
- back_y: float32 [8192, 4096], P('gx', 'gy'), may hold values from -1 to 1
- couple_y: float32 [8192, 4096], P('gx', 'gy'), may hold values from -0.375 to 0.375
Outputs:
- solved_field: float32 [16, 512, 4096], P(None, 'gx', 'gy')
The draws below stay inside these ranges and needn't reach their ends.
All inputs are finite; a program needn't handle non-finite values.
Results may differ from the reference program's by a relative error of at most 0.00012.
Values sent between devices are 32-bit elements; how exact they have to be, the bound alone decides.
A program may use at most 128 MiB of HBM per device.

```python
import math
import jax
import jax.numpy as jnp
from jax import lax

Z = 16
EXC = 16
NCLASS = 8
CX = 16
CY = 16
KX = 256
KY = 256
NX = 512
NY = 256
N_GX = 32
N_GY = 16


def dominant_draw(key, row_count, col_count, block_width):
    rate_key, other_key = jax.random.split(key)
    row_ids = lax.broadcasted_iota(jnp.int32, (row_count, col_count), 0) % block_width
    col_ids = lax.broadcasted_iota(jnp.int32, (row_count, col_count), 1) % block_width
    rates = jax.random.uniform(rate_key, (row_count, col_count), jnp.float32, 0.2, 0.95)
    others = jnp.clip(jax.random.normal(other_key, (row_count, col_count), jnp.float32), -4.0, 4.0) * (0.2 / math.sqrt(block_width))
    return jnp.where(row_ids == col_ids, rates, others)


def draw_fwd_x(key, part):
    return dominant_draw(jax.random.fold_in(key, 11), N_GX * KX, N_GY * KX, KX)


def draw_back_x(key, part):
    return dominant_draw(jax.random.fold_in(key, 12), N_GX * KX, N_GY * KX, KX)


def draw_fwd_y(key, part):
    return dominant_draw(jax.random.fold_in(key, 13), N_GX * KY, N_GY * KY, KY)


def draw_back_y(key, part):
    return dominant_draw(jax.random.fold_in(key, 14), N_GX * KY, N_GY * KY, KY)


def set_ends(drawn, stream_key, least, high):
    spot = [jax.random.randint(jax.random.fold_in(stream_key, axis), (), 0, length) for axis, length in enumerate(drawn.shape)]
    longest = drawn.shape.index(max(drawn.shape))
    next_to = spot[:longest] + [(spot[longest] + 1) % drawn.shape[longest]] + spot[longest + 1:]
    return drawn.at[tuple(spot)].set(least).at[tuple(next_to)].set(high)


def shard_levels(own_key, shape, shards, least, high):
    loudness, own = 1.0, jax.random.fold_in(own_key, 6)
    for axis_at, parts in shards:
        draws = jnp.exp(jax.random.uniform(jax.random.fold_in(own, axis_at), (parts,), jnp.float32, least / len(shards), high / len(shards)))
        loudness = loudness * jnp.repeat(draws, shape[axis_at] // parts).reshape([-1 if axis == axis_at else 1 for axis in range(len(shape))])
    return loudness


def bell_draw(own_key, dims, width, reach, cuts=(), kind=jnp.bfloat16):
    entries = width * jax.random.normal(own_key, dims, jnp.float32)
    if cuts:
        entries = entries * shard_levels(own_key, dims, cuts, -0.22, 0.18)
    return jnp.clip(entries, -reach, reach).astype(kind)


def setup_inputs(seed: int = 0) -> dict:
    seeds = jax.random.split(jax.random.key(seed), 14)
    start_field = bell_draw(seeds[0], (EXC, NX, NY * Z), 1.0, 6.0, ((1, 32), (2, 16)), jnp.float32)
    classes = set_ends(jax.random.randint(seeds[1], (NX, NY * Z), 0, NCLASS), jax.random.fold_in(seeds[1], 1), 0, NCLASS - 1).astype(jnp.int32)
    conductor = set_ends(jax.random.randint(seeds[2], (NX, NY * Z), 0, EXC), jax.random.fold_in(seeds[2], 1), 0, EXC - 1).astype(jnp.int32)
    drive = bell_draw(seeds[3], (NX, NY * Z), 1.0, 6.0, ((0, 32), (1, 16)), jnp.float32)
    perm_table = jnp.clip(jnp.exp(jax.random.uniform(seeds[4], (NCLASS,), jnp.float32, math.log(1.0), math.log(4.0))), 1.0, 4.0)
    leaf_x = bell_draw(seeds[5], (NX, NY * Z), 0.1, 1.5, ((0, 32), (1, 16)), jnp.float32)
    leaf_y = bell_draw(seeds[6], (NX, NY * Z), 0.1, 1.5, ((0, 32), (1, 16)), jnp.float32)
    fwd_x = draw_fwd_x(jax.random.fold_in(seeds[13], 71), 0)
    back_x = draw_back_x(jax.random.fold_in(seeds[13], 71), 0)
    couple_x = bell_draw(seeds[9], (N_GX * KX, N_GY * KX), KX ** -0.5, 0.375, ((0, 32), (1, 16)), jnp.float32)
    fwd_y = draw_fwd_y(jax.random.fold_in(seeds[13], 71), 0)
    back_y = draw_back_y(jax.random.fold_in(seeds[13], 71), 0)
    couple_y = bell_draw(seeds[12], (N_GX * KY, N_GY * KY), KY ** -0.5, 0.375, ((0, 32), (1, 16)), jnp.float32)
    return {"start_field": start_field, "classes": classes, "conductor": conductor, "drive": drive, "perm_table": perm_table, "leaf_x": leaf_x, "leaf_y": leaf_y, "fwd_x": fwd_x, "back_x": back_x, "couple_x": couple_x, "fwd_y": fwd_y, "back_y": back_y, "couple_y": couple_y}


HIGHEST_MODE = lax.Precision.HIGHEST


def residual_of(start_field, classes, conductor, drive, perm_table):
    excites, rows_all, span_all = start_field.shape
    padded_cols = jnp.pad(start_field, ((0, 0), (1, 1), (0, 0)))
    padded_rows = jnp.pad(start_field, ((0, 0), (0, 0), (Z, Z)))
    beside = padded_cols[:, 2:, :] + padded_cols[:, :-2, :] + padded_rows[:, :, 2 * Z:] + padded_rows[:, :, :-2 * Z]
    node_index = lax.broadcasted_iota(jnp.int32, (1, 1, span_all), 2) % Z
    zero_col = jnp.zeros((excites, rows_all, 1), start_field.dtype)
    upper = jnp.where(node_index == Z - 1, 0.0, jnp.concatenate([start_field[:, :, 1:], zero_col], axis=2))
    lower = jnp.where(node_index == 0, 0.0, jnp.concatenate([zero_col, start_field[:, :, :-1]], axis=2))
    permit = perm_table[classes]
    excite_ids = jnp.arange(excites, dtype=jnp.int32)
    source = drive[None] * (conductor[None] == excite_ids[:, None, None]).astype(start_field.dtype)
    return source - (permit[None] * (4.0 * start_field - beside) + 2.0 * start_field - (upper + lower))


def chain_run(matrices, terms, backward):
    def advance(carry, inputs):
        matrix, term = inputs
        following = jnp.einsum('jek,jkl->jel', carry, matrix, precision=HIGHEST_MODE) + term
        return following, following

    final_state, history = lax.scan(advance, jnp.zeros_like(terms[0]), (matrices, terms), reverse=backward)
    return history


def sweep_pair(forward_ops, backward_ops, couple_ops, sources):
    ahead = chain_run(forward_ops, sources, False)
    feed = jnp.einsum('njek,njkl->njel', ahead, couple_ops, precision=HIGHEST_MODE)
    return chain_run(backward_ops, feed, True)


def reference(start_field, classes, conductor, drive, perm_table, leaf_x, leaf_y, fwd_x, back_x, couple_x, fwd_y, back_y, couple_y):
    resid = residual_of(start_field, classes, conductor, drive, perm_table)

    def col_blocks(operator):
        return operator.reshape(N_GX, KX, N_GY, KX).transpose(0, 2, 1, 3)

    def row_blocks(operator):
        return operator.reshape(N_GX, KY, N_GY, KY).transpose(2, 0, 1, 3)

    src_x = (leaf_x[None] * resid).reshape(EXC, N_GX, CX, N_GY, KX).sum(axis=2).transpose(1, 2, 0, 3)
    across_all = sweep_pair(col_blocks(fwd_x), col_blocks(back_x), col_blocks(couple_x), src_x)
    across_flat = across_all.transpose(2, 0, 1, 3).reshape(EXC, N_GX, 1, N_GY * KX)
    across_field = jnp.broadcast_to(across_flat, (EXC, N_GX, CX, N_GY * KX)).reshape(EXC, NX, NY * Z)
    lifted = resid + leaf_x[None] * across_field
    src_y = (lifted * leaf_y[None]).reshape(EXC, NX, N_GY, CY, Z).sum(axis=3)
    src_y = src_y.reshape(EXC, N_GX, CX, N_GY, Z).transpose(3, 1, 0, 2, 4).reshape(N_GY, N_GX, EXC, KY)
    along_all = sweep_pair(row_blocks(fwd_y), row_blocks(back_y), row_blocks(couple_y), src_y)
    along_grid = along_all.reshape(N_GY, N_GX, EXC, CX, Z).transpose(2, 1, 3, 0, 4)
    along_field = jnp.broadcast_to(along_grid[:, :, :, :, None, :], (EXC, N_GX, CX, N_GY, CY, Z)).reshape(EXC, NX, NY * Z)
    return start_field + leaf_x[None] * across_field + leaf_y[None] * along_field
```

```python
import functools

import jax
import jax.numpy as jnp
from jax import lax
from jax.experimental import pallas as pl
from jax.experimental.pallas import tpu as pltpu
from jax.sharding import PartitionSpec as P

Z = 16
E = 16
C = 16
K = 256
NX_DEV = 32
NY_DEV = 16
G = 4
MESH = pl.DeviceIdType.MESH

HALO = 0
FX, BX, FY, BY = 4, 7, 10, 13
SX, QX, SY, QY = 16, 19, 22, 25
EXF, EXB, EYF, EYB = 28, 29, 30, 31
COPIES = 32


def split(x):
    high = x.astype(jnp.bfloat16)
    low = (x - high.astype(jnp.float32)).astype(jnp.bfloat16)
    return high, low


def product(state, wide):
    high, low = split(state)
    r = jnp.dot(
        jnp.concatenate([high, low], axis=0), wide, preferred_element_type=jnp.float32
    )
    return (r[E:, K:] + r[:E, K:] + r[E:, :K]) + r[:E, :K]


def kernel(
    start_ref, classes_ref, conductor_ref, drive_ref, perm_ref, leaf_x_ref, leaf_y_ref,
    fwd_x_ref, back_x_ref, couple_x_ref, fwd_y_ref, back_y_ref, couple_y_ref,
    out_ref,
    edge_out, edge_in, row_in, resid_ref, permit_ref,
    got_x, got_y, wide_x, wide_y, wide_c,
    src_ref, state_out, state_in, across_ref, along_ref,
    send_sem, recv_sem,
):
    i = lax.axis_index("gx")
    j = lax.axis_index("gy")
    ix, gx = i % G, i // G
    jy, gy = j % G, j // G
    core, chip = ix % 2, ix // 2

    def at_x(index):
        return (index, j)

    def at_y(index):
        return (i, index)

    xp = [
        gx * G + 2 * chip + (1 - core),
        gx * G + 2 * (1 - chip) + core,
        gx * G + 2 * (1 - chip) + (1 - core),
    ]
    yp = [gy * G + (jy + d) % G for d in (1, 2, 3)]

    def slot_x(k):
        return 2 * ((chip + k // 2) % 2) + (core + k % 2) % 2

    def slot_y(k):
        return (jy + G - k) % G

    partners = [(None, at_x(p)) for p in xp] + [(None, at_y(p)) for p in yp]
    partners += [
        ((ix == 0) & (i > 0), at_x(i - 1)),
        ((ix == G - 1) & (i < NX_DEV - 1), at_x(i + 1)),
        (i >= G, at_x(i - G)),
        (i < NX_DEV - G, at_x(i + G)),
        ((jy == 0) & (j > 0), at_y(j - 1)),
        ((jy == G - 1) & (j < NY_DEV - 1), at_y(j + 1)),
        (j >= G, at_y(j - G)),
        (j < NY_DEV - G, at_y(j + G)),
    ]
    barrier = pltpu.get_barrier_semaphore()
    for held, where in partners:
        def greet(where=where):
            pl.semaphore_signal(barrier, inc=1, device_id=where, device_id_type=MESH)
        if held is None:
            greet()
        else:
            pl.when(held)(greet)
    edge_out[0] = start_ref[:, C - 1, :]
    edge_out[1] = start_ref[:, 0, :]
    count = 6
    for held, _ in partners[6:]:
        count = count + held.astype(jnp.int32)
    pl.semaphore_wait(barrier, count)

    def copy(src, dst, number, where):
        return pltpu.make_async_remote_copy(
            src_ref=src, dst_ref=dst, send_sem=send_sem.at[number],
            recv_sem=recv_sem.at[number], device_id=where, device_id_type=MESH,
        )

    halo = [
        (i < NX_DEV - 1, i > 0, copy(edge_out.at[0], edge_in.at[0], HALO, at_x(i + 1))),
        (i > 0, i < NX_DEV - 1, copy(edge_out.at[1], edge_in.at[1], HALO + 1, at_x(i - 1))),
        (j < NY_DEV - 1, j > 0,
         copy(start_ref.at[:, :, pl.ds(K // 2, K // 2)], row_in.at[0], HALO + 2, at_y(j + 1))),
        (j > 0, j < NY_DEV - 1,
         copy(start_ref.at[:, :, pl.ds(0, K // 2)], row_in.at[1], HALO + 3, at_y(j - 1))),
    ]
    for sends, _, move in halo:
        pl.when(sends)(move.start)

    ops_x = []
    for n, (ref, number) in enumerate(((fwd_x_ref, FX), (back_x_ref, BX))):
        ops_x.append([
            copy(ref, got_x.at[n, 0], number, at_x(xp[0])),
            copy(ref, got_x.at[n, 1], number + 1, at_x(xp[1])),
            copy(got_x.at[n, 1], got_x.at[n, 2], number + 2, at_x(xp[0])),
        ])
    ops_y = []
    for n, (ref, number) in enumerate(((fwd_y_ref, FY), (back_y_ref, BY))):
        ops_y.append([
            copy(ref, got_y.at[n, d], number + d, at_y(yp[d])) for d in range(3)
        ])
    for n in range(2):
        ops_x[n][1].start()
        ops_x[n][0].start()
    for n in range(2):
        for move in ops_y[n]:
            move.start()

    def widen(ref, target):
        high, low = split(ref[...])
        target[:, :K] = high
        target[:, K:] = low

    widen(couple_x_ref, wide_c.at[0])
    widen(couple_y_ref, wide_c.at[1])
    widen(fwd_x_ref, wide_x.at[0, 0])
    widen(back_x_ref, wide_x.at[1, 0])
    widen(fwd_y_ref, wide_y.at[0, 0])
    widen(back_y_ref, wide_y.at[1, 0])

    permit = jnp.zeros((C, K), jnp.float32)
    for c in range(8):
        permit = jnp.where(classes_ref[...] == c, perm_ref[c], permit)
    permit_ref[...] = permit

    lane = lax.broadcasted_iota(jnp.int32, (C, K), 1)
    col = lax.broadcasted_iota(jnp.int32, (C, K), 0)
    node = lane % Z
    mine = lane // Z == col

    for n, target in ((0, edge_in.at[0]), (1, edge_in.at[1]), (2, row_in.at[0]), (3, row_in.at[1])):
        _, receives, move = halo[n]
        pl.when(receives)(move.wait_recv)

        def clear(target=target):
            target[...] = jnp.zeros(target.shape, jnp.float32)
        pl.when(jnp.logical_not(receives))(clear)

    def residual(e, _):
        x = start_ref[e]
        low = edge_in[0, pl.ds(e, 1), :]
        high = edge_in[1, pl.ds(e, 1), :]
        after = jnp.where(col == C - 1, high, pltpu.roll(x, C - 1, 0))
        before = jnp.where(col == 0, low, pltpu.roll(x, 1, 0))
        piece = row_in[0, e]
        row_before = pltpu.roll(
            jnp.where(lane >= K - Z, jnp.concatenate([piece, piece], axis=1), x), Z, 1)
        piece = row_in[1, e]
        row_after = pltpu.roll(
            jnp.where(lane < Z, jnp.concatenate([piece, piece], axis=1), x), K - Z, 1)
        beside = after + before + row_after + row_before
        upper = jnp.where(node == Z - 1, 0.0, pltpu.roll(x, K - 1, 1))
        lower = jnp.where(node == 0, 0.0, pltpu.roll(x, 1, 1))
        source = jnp.where(conductor_ref[...] == e, drive_ref[...], 0.0)
        resid = source - (permit_ref[...] * (4.0 * x - beside) + 2.0 * x - (upper + lower))
        resid_ref[e] = resid
        src_ref[0, 0, pl.ds(e, 1), :] = jnp.sum(leaf_x_ref[...] * resid, axis=0, keepdims=True)
        return 0

    lax.fori_loop(0, E, residual, 0)

    def share(n, number, places):
        moves = [
            copy(src_ref.at[n, 0], src_ref.at[n, d + 1], number + d, places[d])
            for d in range(3)
        ]
        for move in reversed(moves):
            move.start()
        return moves

    def sweep(n, moves, wide, way, slot, order, position, first, last, number, to):
        for move in moves:
            move.wait_recv()
        step = copy(state_out.at[n], state_in.at[n], number, to)

        def clear():
            state_in[n] = jnp.zeros((E, K), jnp.float32)
        pl.when(first)(clear)
        pl.when(jnp.logical_not(first))(step.wait_recv)
        state = state_in[n]
        kept = jnp.zeros((E, K), jnp.float32)
        for k in order:
            s = slot(k)
            state = product(state, wide[way, s]) + src_ref[n, s]
            kept = jnp.where(position == k, state, kept)
        state_out[n] = state
        pl.when(jnp.logical_not(last))(step.start)
        return kept, step

    up, down = (0, 1, 2, 3), (3, 2, 1, 0)
    x_first, x_last = i < G, i >= NX_DEV - G
    y_first, y_last = j < G, j >= NY_DEV - G
    to_xf = at_x(i + G)
    to_xb = at_x(i - G)

    moves_sx = share(0, SX, [at_x(p) for p in xp])
    for n in range(2):
        ops_x[n][1].wait_recv()
        ops_x[n][2].start()
        widen(got_x.at[n, 1], wide_x.at[n, 2])
        ops_x[n][0].wait_recv()
        widen(got_x.at[n, 0], wide_x.at[n, 1])
        if n == 0:
            ops_x[n][2].wait_recv()
            widen(got_x.at[n, 2], wide_x.at[n, 3])
            ahead, step_xf = sweep(
                0, moves_sx, wide_x, 0, slot_x, up, ix, x_first, x_last, EXF, to_xf)
            src_ref[1, 0] = product(ahead, wide_c[0])
            moves_qx = share(1, QX, [at_x(p) for p in xp])
    ops_x[1][2].wait_recv()
    widen(got_x.at[1, 2], wide_x.at[1, 3])
    across, step_xb = sweep(
        1, moves_qx, wide_x, 1, slot_x, down, ix, x_last, x_first, EXB, to_xb)
    across_ref[...] = across

    def gather_y(e, _):
        lifted = resid_ref[e] + leaf_x_ref[...] * across_ref[pl.ds(e, 1), :]
        t = lifted * leaf_y_ref[...]
        for shift in (128, 64, 32, 16):
            t = t + pltpu.roll(t, shift, 1)
        src_ref[2, 0, pl.ds(e, 1), :] = jnp.sum(jnp.where(mine, t, 0.0), axis=0, keepdims=True)
        return 0

    lax.fori_loop(0, E, gather_y, 0)
    moves_sy = share(2, SY, [at_y(p) for p in yp])
    for n in range(2):
        for d in range(3):
            ops_y[n][d].wait_recv()
            widen(got_y.at[n, d], wide_y.at[n, d + 1])
    ahead, step_yf = sweep(
        2, moves_sy, wide_y, 0, slot_y, up, jy, y_first, y_last, EYF, at_y(j + G))
    src_ref[3, 0] = product(ahead, wide_c[1])
    moves_qy = share(3, QY, [at_y(p) for p in yp])
    along, step_yb = sweep(
        3, moves_qy, wide_y, 1, slot_y, down, jy, y_last, y_first, EYB, at_y(j - G))
    along_ref[...] = along

    def finish(e, _):
        t = jnp.where(mine, along_ref[pl.ds(e, 1), :], 0.0)
        for shift in (128, 64, 32, 16):
            t = t + pltpu.roll(t, shift, 1)
        out_ref[e] = (
            start_ref[e] + leaf_x_ref[...] * across_ref[pl.ds(e, 1), :] + leaf_y_ref[...] * t
        )
        return 0

    lax.fori_loop(0, E, finish, 0)

    for sends, _, move in halo:
        pl.when(sends)(move.wait_send)
    for moves in ops_x + ops_y + [moves_sx, moves_qx, moves_sy, moves_qy]:
        for move in moves:
            move.wait_send()
    pl.when(jnp.logical_not(x_last))(step_xf.wait_send)
    pl.when(jnp.logical_not(x_first))(step_xb.wait_send)
    pl.when(jnp.logical_not(y_last))(step_yf.wait_send)
    pl.when(jnp.logical_not(y_first))(step_yb.wait_send)


def local(*arrays):
    vmem = pl.BlockSpec(memory_space=pltpu.VMEM)
    smem = pl.BlockSpec(memory_space=pltpu.SMEM)
    f32, bf16 = jnp.float32, jnp.bfloat16
    return pl.pallas_call(
        kernel,
        out_shape=jax.ShapeDtypeStruct((E, C, K), f32),
        in_specs=[vmem] * 4 + [smem] + [vmem] * 8,
        out_specs=vmem,
        scratch_shapes=[
            pltpu.VMEM((2, E, K), f32),
            pltpu.VMEM((2, E, K), f32),
            pltpu.VMEM((2, E, C, K // 2), f32),
            pltpu.VMEM((E, C, K), f32),
            pltpu.VMEM((C, K), f32),
            pltpu.VMEM((2, 3, K, K), f32),
            pltpu.VMEM((2, 3, K, K), f32),
            pltpu.VMEM((2, G, K, 2 * K), bf16),
            pltpu.VMEM((2, G, K, 2 * K), bf16),
            pltpu.VMEM((2, K, 2 * K), bf16),
            pltpu.VMEM((4, G, E, K), f32),
            pltpu.VMEM((4, E, K), f32),
            pltpu.VMEM((4, E, K), f32),
            pltpu.VMEM((E, K), f32),
            pltpu.VMEM((E, K), f32),
            pltpu.SemaphoreType.DMA((COPIES,)),
            pltpu.SemaphoreType.DMA((COPIES,)),
        ],
        compiler_params=pltpu.CompilerParams(
            collective_id=0, has_side_effects=True, vmem_limit_bytes=48 * 1024 * 1024
        ),
    )(*arrays)


def solution(mesh):
    split_two = P("gx", "gy")
    in_specs = (P(None, "gx", "gy"),) + (split_two,) * 3 + (P(),) + (split_two,) * 8
    return jax.shard_map(
        local, mesh=mesh, in_specs=in_specs, out_specs=P(None, "gx", "gy"), check_vma=False
    )
```

```python
import functools

import jax
import jax.numpy as jnp
from jax import lax
from jax.experimental import pallas as pl
from jax.experimental.pallas import tpu as pltpu
from jax.sharding import PartitionSpec as P

Z = 16
E = 16
C = 16
K = 256
NX_DEV = 32
NY_DEV = 16
G = 4
MESH = pl.DeviceIdType.MESH

HALO = 0
FX, BX, FY, BY = 4, 7, 10, 13
SX, QX, SY, QY = 16, 19, 22, 25
EXF, EXB, EYF, EYB = 28, 29, 30, 31
COPIES = 32

DOWN, UP = 2.0**-24, 2.0**24
ROWS = 128


def split(x):
    high = x.astype(jnp.bfloat16)
    low = (x - high.astype(jnp.float32)).astype(jnp.bfloat16)
    return high, low


def product_of(high, low, wide):
    rows = high.shape[0]
    r = jnp.dot(
        jnp.concatenate([high, low], axis=0), wide, preferred_element_type=jnp.float32
    )
    return (r[rows:, K:] + r[:rows, K:] + r[rows:, :K]) + r[:rows, :K]


def product(state, wide):
    return product_of(*split(state), wide)


def kernel(
    start_ref, classes_ref, conductor_ref, drive_ref, perm_ref, leaf_x_ref, leaf_y_ref,
    fwd_x_ref, back_x_ref, couple_x_ref, fwd_y_ref, back_y_ref, couple_y_ref,
    out_ref,
    edge_out, edge_in, row_in, resid_ref, permit_ref,
    got_x, got_y, wide_x, wide_y, wide_c, whole_ref, prefix_ref,
    src_ref, kept_ref, tail_ref, state_out, state_in, across_ref, along_ref,
    send_sem, recv_sem,
):
    i = lax.axis_index("gx")
    j = lax.axis_index("gy")
    ix, gx = i % G, i // G
    jy, gy = j % G, j // G
    core, chip = ix % 2, ix // 2

    def at_x(index):
        return (index, j)

    def at_y(index):
        return (i, index)

    xp = [
        gx * G + 2 * chip + (1 - core),
        gx * G + 2 * (1 - chip) + core,
        gx * G + 2 * (1 - chip) + (1 - core),
    ]
    yp = [gy * G + (jy + d) % G for d in (1, 2, 3)]

    def slot_x(k):
        return 2 * ((chip + k // 2) % 2) + (core + k % 2) % 2

    def slot_y(k):
        return (jy + G - k) % G

    partners = [(None, at_x(p)) for p in xp] + [(None, at_y(p)) for p in yp]
    partners += [
        ((ix == 0) & (i > 0), at_x(i - 1)),
        ((ix == G - 1) & (i < NX_DEV - 1), at_x(i + 1)),
        (i >= G, at_x(i - G)),
        (i < NX_DEV - G, at_x(i + G)),
        ((jy == 0) & (j > 0), at_y(j - 1)),
        ((jy == G - 1) & (j < NY_DEV - 1), at_y(j + 1)),
        (j >= G, at_y(j - G)),
        (j < NY_DEV - G, at_y(j + G)),
    ]
    barrier = pltpu.get_barrier_semaphore()
    for held, where in partners:
        def greet(where=where):
            pl.semaphore_signal(barrier, inc=1, device_id=where, device_id_type=MESH)
        if held is None:
            greet()
        else:
            pl.when(held)(greet)
    edge_out[0] = start_ref[:, C - 1, :]
    edge_out[1] = start_ref[:, 0, :]
    count = 6
    for held, _ in partners[6:]:
        count = count + held.astype(jnp.int32)
    pl.semaphore_wait(barrier, count)

    def copy(src, dst, number, where):
        return pltpu.make_async_remote_copy(
            src_ref=src, dst_ref=dst, send_sem=send_sem.at[number],
            recv_sem=recv_sem.at[number], device_id=where, device_id_type=MESH,
        )

    halo = [
        (i < NX_DEV - 1, i > 0, copy(edge_out.at[0], edge_in.at[0], HALO, at_x(i + 1))),
        (i > 0, i < NX_DEV - 1, copy(edge_out.at[1], edge_in.at[1], HALO + 1, at_x(i - 1))),
        (j < NY_DEV - 1, j > 0,
         copy(start_ref.at[:, :, pl.ds(K // 2, K // 2)], row_in.at[0], HALO + 2, at_y(j + 1))),
        (j > 0, j < NY_DEV - 1,
         copy(start_ref.at[:, :, pl.ds(0, K // 2)], row_in.at[1], HALO + 3, at_y(j - 1))),
    ]
    for sends, _, move in halo:
        pl.when(sends)(move.start)

    ops_x = []
    for n, (ref, number) in enumerate(((fwd_x_ref, FX), (back_x_ref, BX))):
        ops_x.append([
            copy(ref, got_x.at[n, 0], number, at_x(xp[0])),
            copy(ref, got_x.at[n, 1], number + 1, at_x(xp[1])),
            copy(got_x.at[n, 1], got_x.at[n, 2], number + 2, at_x(xp[0])),
        ])
    ops_y = []
    for n, (ref, number) in enumerate(((fwd_y_ref, FY), (back_y_ref, BY))):
        ops_y.append([
            copy(ref, got_y.at[n, d], number + d, at_y(yp[d])) for d in range(3)
        ])
    for n in range(2):
        ops_x[n][1].start()
        ops_x[n][0].start()
    for n in range(2):
        for move in ops_y[n]:
            move.start()

    def widen(ref, target):
        high, low = split(ref[...])
        target[:, :K] = high
        target[:, K:] = low

    widen(couple_x_ref, wide_c.at[0])
    widen(couple_y_ref, wide_c.at[1])
    widen(fwd_x_ref, wide_x.at[0, 0])
    widen(back_x_ref, wide_x.at[1, 0])
    widen(fwd_y_ref, wide_y.at[0, 0])
    widen(back_y_ref, wide_y.at[1, 0])

    permit = jnp.zeros((C, K), jnp.float32)
    for c in range(8):
        permit = jnp.where(classes_ref[...] == c, perm_ref[c], permit)
    permit_ref[...] = permit

    lane = lax.broadcasted_iota(jnp.int32, (C, K), 1)
    col = lax.broadcasted_iota(jnp.int32, (C, K), 0)
    node = lane % Z
    mine = lane // Z == col

    for n, target in ((0, edge_in.at[0]), (1, edge_in.at[1]), (2, row_in.at[0]), (3, row_in.at[1])):
        _, receives, move = halo[n]
        pl.when(receives)(move.wait_recv)

        def clear(target=target):
            target[...] = jnp.zeros(target.shape, jnp.float32)
        pl.when(jnp.logical_not(receives))(clear)

    def residual(e, _):
        x = start_ref[e]
        low = edge_in[0, pl.ds(e, 1), :]
        high = edge_in[1, pl.ds(e, 1), :]
        after = jnp.where(col == C - 1, high, pltpu.roll(x, C - 1, 0))
        before = jnp.where(col == 0, low, pltpu.roll(x, 1, 0))
        piece = row_in[0, e]
        row_before = pltpu.roll(
            jnp.where(lane >= K - Z, jnp.concatenate([piece, piece], axis=1), x), Z, 1)
        piece = row_in[1, e]
        row_after = pltpu.roll(
            jnp.where(lane < Z, jnp.concatenate([piece, piece], axis=1), x), K - Z, 1)
        beside = after + before + row_after + row_before
        upper = jnp.where(node == Z - 1, 0.0, pltpu.roll(x, K - 1, 1))
        lower = jnp.where(node == 0, 0.0, pltpu.roll(x, 1, 1))
        source = jnp.where(conductor_ref[...] == e, drive_ref[...], 0.0)
        resid = source - (permit_ref[...] * (4.0 * x - beside) + 2.0 * x - (upper + lower))
        resid_ref[e] = resid
        src_ref[0, 0, pl.ds(e, 1), :] = jnp.sum(leaf_x_ref[...] * resid, axis=0, keepdims=True)
        return 0

    lax.fori_loop(0, E, residual, 0)

    def share(n, number, places):
        moves = [
            copy(src_ref.at[n, 0], src_ref.at[n, d + 1], number + d, places[d])
            for d in range(3)
        ]
        for move in reversed(moves):
            move.start()
        return moves

    def compose(n, wide, way, slot, order, position):
        def part(h, _):
            rows = pl.ds(pl.multiple_of(h * ROWS, ROWS), ROWS)

            def put(target, x):
                high, low = split(x * DOWN)
                target[n, rows, :K] = high
                target[n, rows, K:] = low

            pair = wide[way, slot(order[0]), rows, :]
            high, low = pair[:, :K], pair[:, K:]
            x = high.astype(jnp.float32) + low.astype(jnp.float32)
            pl.when(position == order[0])(functools.partial(put, prefix_ref, x))
            for k in order[1:]:
                x = product_of(high, low, wide[way, slot(k)])
                pl.when(position == k)(functools.partial(put, prefix_ref, x))
                high, low = split(x)
            put(whole_ref, x)
            return 0

        lax.fori_loop(0, K // ROWS, part, 0)

    def step_of(n, number, to):
        return copy(state_out.at[n], state_in.at[n], number, to)

    def inside(n, moves, wide, way, slot, order, position, first, step):
        for move in moves:
            move.wait_recv()
        state = src_ref[n, slot(order[0])] * DOWN
        kept = state
        for k in order[1:]:
            s = slot(k)
            state = product(state, wide[way, s]) + src_ref[n, s] * DOWN
            kept = jnp.where(position == k, state, kept)
        kept_ref[n] = kept
        tail_ref[n] = state

        def begin():
            state_out[n] = state * UP
            step.start()
            state_in[n] = jnp.zeros((E, K), jnp.float32)
        pl.when(first)(begin)

    def across_groups(n, first, last, step):
        def take():
            step.wait_recv()
        pl.when(jnp.logical_not(first))(take)

        def give():
            state_out[n] = (product(state_in[n], whole_ref[n]) + tail_ref[n]) * UP
            step.start()
        pl.when(jnp.logical_not(first) & jnp.logical_not(last))(give)
        return (product(state_in[n], prefix_ref[n]) + kept_ref[n]) * UP

    up, down = (0, 1, 2, 3), (3, 2, 1, 0)
    x_first, x_last = i < G, i >= NX_DEV - G
    y_first, y_last = j < G, j >= NY_DEV - G
    step_xf = step_of(0, EXF, at_x(i + G))
    step_xb = step_of(1, EXB, at_x(i - G))
    step_yf = step_of(2, EYF, at_y(j + G))
    step_yb = step_of(3, EYB, at_y(j - G))
    early = i < NX_DEV // 2
    late = jnp.logical_not(early)

    def receive_x(n):
        ops_x[n][1].wait_recv()
        ops_x[n][2].start()
        widen(got_x.at[n, 1], wide_x.at[n, 2])
        ops_x[n][0].wait_recv()
        widen(got_x.at[n, 0], wide_x.at[n, 1])
        ops_x[n][2].wait_recv()
        widen(got_x.at[n, 2], wide_x.at[n, 3])

    def ready_back_x():
        receive_x(1)
        compose(1, wide_x, 1, slot_x, down, ix)

    def ready_y():
        for n, order in ((0, up), (1, down)):
            for d in range(3):
                ops_y[n][d].wait_recv()
                widen(got_y.at[n, d], wide_y.at[n, d + 1])
            compose(2 + n, wide_y, n, slot_y, order, jy)

    moves_sx = share(0, SX, [at_x(p) for p in xp])
    receive_x(0)
    inside(0, moves_sx, wide_x, 0, slot_x, up, ix, x_first, step_xf)
    compose(0, wide_x, 0, slot_x, up, ix)
    pl.when(late)(ready_back_x)
    ahead = across_groups(0, x_first, x_last, step_xf)
    src_ref[1, 0] = product(ahead, wide_c[0])
    moves_qx = share(1, QX, [at_x(p) for p in xp])
    pl.when(early)(ready_back_x)
    inside(1, moves_qx, wide_x, 1, slot_x, down, ix, x_last, step_xb)
    pl.when(early)(ready_y)
    across_ref[...] = across_groups(1, x_last, x_first, step_xb)

    def gather_y(e, _):
        lifted = resid_ref[e] + leaf_x_ref[...] * across_ref[pl.ds(e, 1), :]
        t = lifted * leaf_y_ref[...]
        for shift in (128, 64, 32, 16):
            t = t + pltpu.roll(t, shift, 1)
        src_ref[2, 0, pl.ds(e, 1), :] = jnp.sum(jnp.where(mine, t, 0.0), axis=0, keepdims=True)
        return 0

    lax.fori_loop(0, E, gather_y, 0)
    moves_sy = share(2, SY, [at_y(p) for p in yp])
    pl.when(late)(ready_y)
    inside(2, moves_sy, wide_y, 0, slot_y, up, jy, y_first, step_yf)
    ahead = across_groups(2, y_first, y_last, step_yf)
    src_ref[3, 0] = product(ahead, wide_c[1])
    moves_qy = share(3, QY, [at_y(p) for p in yp])
    inside(3, moves_qy, wide_y, 1, slot_y, down, jy, y_last, step_yb)
    along_ref[...] = across_groups(3, y_last, y_first, step_yb)

    def finish(e, _):
        t = jnp.where(mine, along_ref[pl.ds(e, 1), :], 0.0)
        for shift in (128, 64, 32, 16):
            t = t + pltpu.roll(t, shift, 1)
        out_ref[e] = (
            start_ref[e] + leaf_x_ref[...] * across_ref[pl.ds(e, 1), :] + leaf_y_ref[...] * t
        )
        return 0

    lax.fori_loop(0, E, finish, 0)

    for sends, _, move in halo:
        pl.when(sends)(move.wait_send)
    for moves in ops_x + ops_y + [moves_sx, moves_qx, moves_sy, moves_qy]:
        for move in moves:
            move.wait_send()
    pl.when(jnp.logical_not(x_last))(step_xf.wait_send)
    pl.when(jnp.logical_not(x_first))(step_xb.wait_send)
    pl.when(jnp.logical_not(y_last))(step_yf.wait_send)
    pl.when(jnp.logical_not(y_first))(step_yb.wait_send)


def local(*arrays):
    vmem = pl.BlockSpec(memory_space=pltpu.VMEM)
    smem = pl.BlockSpec(memory_space=pltpu.SMEM)
    f32, bf16 = jnp.float32, jnp.bfloat16
    return pl.pallas_call(
        kernel,
        out_shape=jax.ShapeDtypeStruct((E, C, K), f32),
        in_specs=[vmem] * 4 + [smem] + [vmem] * 8,
        out_specs=vmem,
        scratch_shapes=[
            pltpu.VMEM((2, E, K), f32),
            pltpu.VMEM((2, E, K), f32),
            pltpu.VMEM((2, E, C, K // 2), f32),
            pltpu.VMEM((E, C, K), f32),
            pltpu.VMEM((C, K), f32),
            pltpu.VMEM((2, 3, K, K), f32),
            pltpu.VMEM((2, 3, K, K), f32),
            pltpu.VMEM((2, G, K, 2 * K), bf16),
            pltpu.VMEM((2, G, K, 2 * K), bf16),
            pltpu.VMEM((2, K, 2 * K), bf16),
            pltpu.VMEM((4, K, 2 * K), bf16),
            pltpu.VMEM((4, K, 2 * K), bf16),
            pltpu.VMEM((4, G, E, K), f32),
            pltpu.VMEM((4, E, K), f32),
            pltpu.VMEM((4, E, K), f32),
            pltpu.VMEM((4, E, K), f32),
            pltpu.VMEM((4, E, K), f32),
            pltpu.VMEM((E, K), f32),
            pltpu.VMEM((E, K), f32),
            pltpu.SemaphoreType.DMA((COPIES,)),
            pltpu.SemaphoreType.DMA((COPIES,)),
        ],
        compiler_params=pltpu.CompilerParams(
            collective_id=0, has_side_effects=True, vmem_limit_bytes=48 * 1024 * 1024
        ),
    )(*arrays)


def solution(mesh):
    split_two = P("gx", "gy")
    in_specs = (P(None, "gx", "gy"),) + (split_two,) * 3 + (P(),) + (split_two,) * 8
    return jax.shard_map(
        local, mesh=mesh, in_specs=in_specs, out_specs=P(None, "gx", "gy"), check_vma=False
    )
```

```python
import functools

import jax
import jax.numpy as jnp
from jax import lax
from jax.experimental import pallas as pl
from jax.experimental.pallas import tpu as pltpu
from jax.sharding import PartitionSpec as P

Z = 16
E = 16
C = 16
K = 256
NX_DEV = 32
NY_DEV = 16
G = 4
MESH = pl.DeviceIdType.MESH

HALO = 0
FX, BX, FY, BY = 4, 7, 10, 13
SX, QX, SY, QY = 16, 19, 22, 25
EXF, EXB = 28, 29
WY = 30
TY = 36
COPIES = 48
WHOLE_PAIRS = ((1, 2), (1, 3), (2, 3))
TAIL_PAIRS = ((0, 1), (0, 2), (0, 3), (1, 2), (1, 3), (2, 3))

DOWN, UP = 2.0**-24, 2.0**24
ROWS = 128


def split(x):
    high = x.astype(jnp.bfloat16)
    low = (x - high.astype(jnp.float32)).astype(jnp.bfloat16)
    return high, low


def product_of(high, low, wide):
    rows = high.shape[0]
    r = jnp.dot(
        jnp.concatenate([high, low], axis=0), wide, preferred_element_type=jnp.float32
    )
    return (r[rows:, K:] + r[:rows, K:] + r[rows:, :K]) + r[:rows, :K]


def product(state, wide):
    return product_of(*split(state), wide)


def kernel(
    start_ref, classes_ref, conductor_ref, drive_ref, perm_ref, leaf_x_ref, leaf_y_ref,
    fwd_x_ref, back_x_ref, couple_x_ref, fwd_y_ref, back_y_ref, couple_y_ref,
    out_ref,
    edge_out, edge_in, row_in, resid_ref, permit_ref,
    got_x, got_y, wide_x, wide_y, wide_c, whole_ref, prefix_ref, whole_out, whole_in, wide_in,
    src_ref, kept_ref, tail_ref, state_out, state_in, tails_in, across_ref, along_ref,
    send_sem, recv_sem,
):
    i = lax.axis_index("gx")
    j = lax.axis_index("gy")
    ix, gx = i % G, i // G
    jy, gy = j % G, j // G
    core, chip = ix % 2, ix // 2

    def at_x(index):
        return (index, j)

    def at_y(index):
        return (i, index)

    xp = [
        gx * G + 2 * chip + (1 - core),
        gx * G + 2 * (1 - chip) + core,
        gx * G + 2 * (1 - chip) + (1 - core),
    ]
    yp = [gy * G + (jy + d) % G for d in (1, 2, 3)]

    def slot_x(k):
        return 2 * ((chip + k // 2) % 2) + (core + k % 2) % 2

    def slot_y(k):
        return (jy + G - k) % G

    partners = [(None, at_x(p)) for p in xp] + [(None, at_y(p)) for p in yp]
    partners += [(None, at_y((gy + q) % G * G + jy)) for q in (1, 2, 3)]
    partners += [
        ((ix == 0) & (i > 0), at_x(i - 1)),
        ((ix == G - 1) & (i < NX_DEV - 1), at_x(i + 1)),
        (i >= G, at_x(i - G)),
        (i < NX_DEV - G, at_x(i + G)),
        ((jy == 0) & (j > 0), at_y(j - 1)),
        ((jy == G - 1) & (j < NY_DEV - 1), at_y(j + 1)),
    ]
    barrier = pltpu.get_barrier_semaphore()
    for held, where in partners:
        def greet(where=where):
            pl.semaphore_signal(barrier, inc=1, device_id=where, device_id_type=MESH)
        if held is None:
            greet()
        else:
            pl.when(held)(greet)
    edge_out[0] = start_ref[:, C - 1, :]
    edge_out[1] = start_ref[:, 0, :]
    count = 9
    for held, _ in partners[9:]:
        count = count + held.astype(jnp.int32)
    pl.semaphore_wait(barrier, count)

    def copy(src, dst, number, where):
        return pltpu.make_async_remote_copy(
            src_ref=src, dst_ref=dst, send_sem=send_sem.at[number],
            recv_sem=recv_sem.at[number], device_id=where, device_id_type=MESH,
        )

    halo = [
        (i < NX_DEV - 1, i > 0, copy(edge_out.at[0], edge_in.at[0], HALO, at_x(i + 1))),
        (i > 0, i < NX_DEV - 1, copy(edge_out.at[1], edge_in.at[1], HALO + 1, at_x(i - 1))),
        (j < NY_DEV - 1, j > 0,
         copy(start_ref.at[:, :, pl.ds(K // 2, K // 2)], row_in.at[0], HALO + 2, at_y(j + 1))),
        (j > 0, j < NY_DEV - 1,
         copy(start_ref.at[:, :, pl.ds(0, K // 2)], row_in.at[1], HALO + 3, at_y(j - 1))),
    ]
    for sends, _, move in halo:
        pl.when(sends)(move.start)

    ops_x = []
    for n, (ref, number) in enumerate(((fwd_x_ref, FX), (back_x_ref, BX))):
        ops_x.append([
            copy(ref, got_x.at[n, 0], number, at_x(xp[0])),
            copy(ref, got_x.at[n, 1], number + 1, at_x(xp[1])),
            copy(got_x.at[n, 1], got_x.at[n, 2], number + 2, at_x(xp[0])),
        ])
    ops_y = []
    for n, (ref, number) in enumerate(((fwd_y_ref, FY), (back_y_ref, BY))):
        ops_y.append([
            copy(ref, got_y.at[n, d], number + d, at_y(yp[d])) for d in range(3)
        ])
    ops_x[0][1].start()
    ops_x[0][0].start()

    def widen(ref, target):
        high, low = split(ref[...])
        target[:, :K] = high
        target[:, K:] = low

    widen(couple_x_ref, wide_c.at[0])
    widen(couple_y_ref, wide_c.at[1])
    widen(fwd_x_ref, wide_x.at[0, 0])
    widen(back_x_ref, wide_x.at[1, 0])
    widen(fwd_y_ref, wide_y.at[0, 0])
    widen(back_y_ref, wide_y.at[1, 0])

    permit = jnp.zeros((C, K), jnp.float32)
    for c in range(8):
        permit = jnp.where(classes_ref[...] == c, perm_ref[c], permit)
    permit_ref[...] = permit

    lane = lax.broadcasted_iota(jnp.int32, (C, K), 1)
    col = lax.broadcasted_iota(jnp.int32, (C, K), 0)
    node = lane % Z
    mine = lane // Z == col

    for n, target in ((0, edge_in.at[0]), (1, edge_in.at[1]), (2, row_in.at[0]), (3, row_in.at[1])):
        _, receives, move = halo[n]
        pl.when(receives)(move.wait_recv)

        def clear(target=target):
            target[...] = jnp.zeros(target.shape, jnp.float32)
        pl.when(jnp.logical_not(receives))(clear)

    def residual(e, _):
        x = start_ref[e]
        low = edge_in[0, pl.ds(e, 1), :]
        high = edge_in[1, pl.ds(e, 1), :]
        after = jnp.where(col == C - 1, high, pltpu.roll(x, C - 1, 0))
        before = jnp.where(col == 0, low, pltpu.roll(x, 1, 0))
        piece = row_in[0, e]
        row_before = pltpu.roll(
            jnp.where(lane >= K - Z, jnp.concatenate([piece, piece], axis=1), x), Z, 1)
        piece = row_in[1, e]
        row_after = pltpu.roll(
            jnp.where(lane < Z, jnp.concatenate([piece, piece], axis=1), x), K - Z, 1)
        beside = after + before + row_after + row_before
        upper = jnp.where(node == Z - 1, 0.0, pltpu.roll(x, K - 1, 1))
        lower = jnp.where(node == 0, 0.0, pltpu.roll(x, 1, 1))
        source = jnp.where(conductor_ref[...] == e, drive_ref[...], 0.0)
        resid = source - (permit_ref[...] * (4.0 * x - beside) + 2.0 * x - (upper + lower))
        resid_ref[e] = resid
        src_ref[0, 0, pl.ds(e, 1), :] = jnp.sum(leaf_x_ref[...] * resid, axis=0, keepdims=True)
        return 0

    lax.fori_loop(0, E, residual, 0)

    def share(n, number, places):
        moves = [
            copy(src_ref.at[n, 0], src_ref.at[n, d + 1], number + d, places[d])
            for d in range(3)
        ]
        for move in reversed(moves):
            move.start()
        return moves

    def compose(n, wide, way, slot, order, position):
        def part(h, _):
            rows = pl.ds(pl.multiple_of(h * ROWS, ROWS), ROWS)

            def put(target, x):
                high, low = split(x * DOWN)
                target[n, rows, :K] = high
                target[n, rows, K:] = low

            pair = wide[way, slot(order[0]), rows, :]
            high, low = pair[:, :K], pair[:, K:]
            x = high.astype(jnp.float32) + low.astype(jnp.float32)
            pl.when(position == order[0])(functools.partial(put, prefix_ref, x))
            for k in order[1:]:
                x = product_of(high, low, wide[way, slot(k)])
                pl.when(position == k)(functools.partial(put, prefix_ref, x))
                high, low = split(x)
            put(whole_ref, x)
            if n >= 2:
                whole_out[n - 2, rows, :] = x * DOWN
            return 0

        lax.fori_loop(0, K // ROWS, part, 0)

    def step_of(n, number, to):
        return copy(state_out.at[n], state_in.at[n], number, to)

    def inside(n, moves, wide, way, slot, order, position, first=None, step=None):
        for move in moves:
            move.wait_recv()
        state = src_ref[n, slot(order[0])] * DOWN
        kept = state
        for k in order[1:]:
            s = slot(k)
            state = product(state, wide[way, s]) + src_ref[n, s] * DOWN
            kept = jnp.where(position == k, state, kept)
        kept_ref[n] = kept
        if step is None:
            state_out[n] = state
            for a, _, move in tails[n - 2]:
                pl.when(rank[n - 2] == a)(move.start)
            return
        tail_ref[n] = state

        def begin():
            state_out[n] = state * UP
            step.start()
            state_in[n] = jnp.zeros((E, K), jnp.float32)
        pl.when(first)(begin)

    def across_groups(n, first, last, step):
        def take():
            step.wait_recv()
        pl.when(jnp.logical_not(first))(take)

        def give():
            state_out[n] = (product(state_in[n], whole_ref[n]) + tail_ref[n]) * UP
            step.start()
        pl.when(jnp.logical_not(first) & jnp.logical_not(last))(give)
        return (product(state_in[n], prefix_ref[n]) + kept_ref[n]) * UP

    def entry_y(n):
        state_in[n] = jnp.zeros((E, K), jnp.float32)
        for place in range(3):
            def take(place=place):
                for a, b, move in tails[n - 2]:
                    if a == place:
                        pl.when(rank[n - 2] == b)(move.wait_recv)
                state = tails_in[n - 2, place]
                if place:
                    state = product(state_in[n], wide_in[n - 2, place - 1]) + state
                state_in[n] = state * UP
            pl.when(rank[n - 2] > place)(take)
        return (product(state_in[n], prefix_ref[n]) + kept_ref[n]) * UP

    rank = (gy, G - 1 - gy)

    def member(way, place):
        return at_y((place if way == 0 else G - 1 - place) * G + jy)

    wholes = [
        [(a, b, copy(whole_out.at[n], whole_in.at[n, a - 1], WY + 3 * n + q, member(n, b)))
         for q, (a, b) in enumerate(WHOLE_PAIRS)]
        for n in range(2)
    ]
    tails = [
        [(a, b, copy(state_out.at[2 + n], tails_in.at[n, a], TY + 6 * n + q, member(n, b)))
         for q, (a, b) in enumerate(TAIL_PAIRS)]
        for n in range(2)
    ]
    up, down = (0, 1, 2, 3), (3, 2, 1, 0)
    x_first, x_last = i < G, i >= NX_DEV - G
    step_xf = step_of(0, EXF, at_x(i + G))
    step_xb = step_of(1, EXB, at_x(i - G))
    early = i < NX_DEV // 2
    late = jnp.logical_not(early)
    before = i < NX_DEV - 2 * G

    def receive_x(n):
        ops_x[n][1].wait_recv()
        ops_x[n][2].start()
        widen(got_x.at[n, 1], wide_x.at[n, 2])
        ops_x[n][0].wait_recv()
        widen(got_x.at[n, 0], wide_x.at[n, 1])
        ops_x[n][2].wait_recv()
        widen(got_x.at[n, 2], wide_x.at[n, 3])

    def ready_back_x():
        receive_x(1)
        compose(1, wide_x, 1, slot_x, down, ix)

    def ready_y():
        for n, order in ((0, up), (1, down)):
            for d in range(3):
                ops_y[n][d].wait_recv()
                widen(got_y.at[n, d], wide_y.at[n, d + 1])
            compose(2 + n, wide_y, n, slot_y, order, jy)
            for a, _, move in wholes[n]:
                pl.when(rank[n] == a)(move.start)
        for n in range(2):
            for a, b, move in wholes[n]:
                def take(a=a, move=move, n=n):
                    move.wait_recv()
                    widen(whole_in.at[n, a - 1], wide_in.at[n, a - 1])
                pl.when(rank[n] == b)(take)

    moves_sx = share(0, SX, [at_x(p) for p in xp])
    receive_x(0)
    inside(0, moves_sx, wide_x, 0, slot_x, up, ix, x_first, step_xf)
    ops_x[1][1].start()
    ops_x[1][0].start()
    for n in range(2):
        for move in ops_y[n]:
            move.start()
    compose(0, wide_x, 0, slot_x, up, ix)
    pl.when(late)(ready_back_x)
    ahead = across_groups(0, x_first, x_last, step_xf)
    src_ref[1, 0] = product(ahead, wide_c[0])
    moves_qx = share(1, QX, [at_x(p) for p in xp])
    pl.when(early)(ready_back_x)
    inside(1, moves_qx, wide_x, 1, slot_x, down, ix, x_last, step_xb)
    pl.when(before)(ready_y)
    across_ref[...] = across_groups(1, x_last, x_first, step_xb)

    def gather_y(e, _):
        lifted = resid_ref[e] + leaf_x_ref[...] * across_ref[pl.ds(e, 1), :]
        t = lifted * leaf_y_ref[...]
        for shift in (128, 64, 32, 16):
            t = t + pltpu.roll(t, shift, 1)
        src_ref[2, 0, pl.ds(e, 1), :] = jnp.sum(jnp.where(mine, t, 0.0), axis=0, keepdims=True)
        return 0

    lax.fori_loop(0, E, gather_y, 0)
    moves_sy = share(2, SY, [at_y(p) for p in yp])
    pl.when(jnp.logical_not(before))(ready_y)
    inside(2, moves_sy, wide_y, 0, slot_y, up, jy)
    ahead = entry_y(2)
    src_ref[3, 0] = product(ahead, wide_c[1])
    moves_qy = share(3, QY, [at_y(p) for p in yp])
    inside(3, moves_qy, wide_y, 1, slot_y, down, jy)
    along_ref[...] = entry_y(3)

    def finish(e, _):
        t = jnp.where(mine, along_ref[pl.ds(e, 1), :], 0.0)
        for shift in (128, 64, 32, 16):
            t = t + pltpu.roll(t, shift, 1)
        out_ref[e] = (
            start_ref[e] + leaf_x_ref[...] * across_ref[pl.ds(e, 1), :] + leaf_y_ref[...] * t
        )
        return 0

    lax.fori_loop(0, E, finish, 0)

    for sends, _, move in halo:
        pl.when(sends)(move.wait_send)
    for moves in ops_x + ops_y + [moves_sx, moves_qx, moves_sy, moves_qy]:
        for move in moves:
            move.wait_send()
    pl.when(jnp.logical_not(x_last))(step_xf.wait_send)
    pl.when(jnp.logical_not(x_first))(step_xb.wait_send)
    for n in range(2):
        for a, _, move in wholes[n] + tails[n]:
            pl.when(rank[n] == a)(move.wait_send)


def local(*arrays):
    vmem = pl.BlockSpec(memory_space=pltpu.VMEM)
    smem = pl.BlockSpec(memory_space=pltpu.SMEM)
    f32, bf16 = jnp.float32, jnp.bfloat16
    return pl.pallas_call(
        kernel,
        out_shape=jax.ShapeDtypeStruct((E, C, K), f32),
        in_specs=[vmem] * 4 + [smem] + [vmem] * 8,
        out_specs=vmem,
        scratch_shapes=[
            pltpu.VMEM((2, E, K), f32),
            pltpu.VMEM((2, E, K), f32),
            pltpu.VMEM((2, E, C, K // 2), f32),
            pltpu.VMEM((E, C, K), f32),
            pltpu.VMEM((C, K), f32),
            pltpu.VMEM((2, 3, K, K), f32),
            pltpu.VMEM((2, 3, K, K), f32),
            pltpu.VMEM((2, G, K, 2 * K), bf16),
            pltpu.VMEM((2, G, K, 2 * K), bf16),
            pltpu.VMEM((2, K, 2 * K), bf16),
            pltpu.VMEM((4, K, 2 * K), bf16),
            pltpu.VMEM((4, K, 2 * K), bf16),
            pltpu.VMEM((2, K, K), f32),
            pltpu.VMEM((2, 2, K, K), f32),
            pltpu.VMEM((2, 2, K, 2 * K), bf16),
            pltpu.VMEM((4, G, E, K), f32),
            pltpu.VMEM((4, E, K), f32),
            pltpu.VMEM((4, E, K), f32),
            pltpu.VMEM((4, E, K), f32),
            pltpu.VMEM((4, E, K), f32),
            pltpu.VMEM((2, 3, E, K), f32),
            pltpu.VMEM((E, K), f32),
            pltpu.VMEM((E, K), f32),
            pltpu.SemaphoreType.DMA((COPIES,)),
            pltpu.SemaphoreType.DMA((COPIES,)),
        ],
        compiler_params=pltpu.CompilerParams(
            collective_id=0, has_side_effects=True, vmem_limit_bytes=48 * 1024 * 1024
        ),
    )(*arrays)


def solution(mesh):
    split_two = P("gx", "gy")
    in_specs = (P(None, "gx", "gy"),) + (split_two,) * 3 + (P(),) + (split_two,) * 8
    return jax.shard_map(
        local, mesh=mesh, in_specs=in_specs, out_specs=P(None, "gx", "gy"), check_vma=False
    )
```

```python
import functools

import jax
import jax.numpy as jnp
from jax import lax
from jax.experimental import pallas as pl
from jax.experimental.pallas import tpu as pltpu
from jax.sharding import PartitionSpec as P

Z = 16
E = 16
C = 16
K = 256
NX_DEV = 32
NY_DEV = 16
G = 4
MESH = pl.DeviceIdType.MESH

HALO = 0
FX, BX, FY, BY = 4, 7, 10, 13
SX, QX, SY, QY = 16, 19, 22, 25
EXF, EXB = 28, 29
WY = 30
TY = 36
COPIES = 48
WHOLE_PAIRS = ((1, 2), (1, 3), (2, 3))
TAIL_PAIRS = ((0, 1), (0, 2), (0, 3), (1, 2), (1, 3), (2, 3))

DOWN, UP = 2.0**-24, 2.0**24
ROWS = 128


def split(x):
    high = x.astype(jnp.bfloat16)
    low = (x - high.astype(jnp.float32)).astype(jnp.bfloat16)
    return high, low


def product_of(high, low, wide):
    rows = high.shape[0]
    r = jnp.dot(
        jnp.concatenate([high, low], axis=0), wide, preferred_element_type=jnp.float32
    )
    return (r[rows:, K:] + r[:rows, K:] + r[rows:, :K]) + r[:rows, :K]


def product(state, wide):
    return product_of(*split(state), wide)


def kernel(
    start_ref, classes_ref, conductor_ref, drive_ref, perm_ref, leaf_x_ref, leaf_y_ref,
    fwd_x_hbm, back_x_hbm, couple_x_hbm, fwd_y_hbm, back_y_hbm, couple_y_hbm,
    out_ref,
    own_ref,
    edge_out, edge_in, row_in, resid_ref, permit_ref,
    got_x, got_y, wide_x, wide_y, wide_c, whole_ref, prefix_ref, whole_out, whole_in, wide_in,
    src_ref, kept_ref, tail_ref, state_out, state_in, tails_in, across_ref, along_ref,
    send_sem, recv_sem, own_sem,
):
    fetches = [
        pltpu.make_async_copy(ref, own_ref.at[n], own_sem.at[n])
        for n, ref in enumerate(
            (fwd_x_hbm, couple_x_hbm, couple_y_hbm, back_x_hbm, fwd_y_hbm, back_y_hbm))
    ]
    for move in fetches:
        move.start()
    fwd_x_ref, couple_x_ref, couple_y_ref, back_x_ref, fwd_y_ref, back_y_ref = (
        own_ref.at[n] for n in range(6))
    i = lax.axis_index("gx")
    j = lax.axis_index("gy")
    ix, gx = i % G, i // G
    jy, gy = j % G, j // G
    core, chip = ix % 2, ix // 2

    def at_x(index):
        return (index, j)

    def at_y(index):
        return (i, index)

    xp = [
        gx * G + 2 * chip + (1 - core),
        gx * G + 2 * (1 - chip) + core,
        gx * G + 2 * (1 - chip) + (1 - core),
    ]
    yp = [gy * G + (jy + d) % G for d in (1, 2, 3)]

    def slot_x(k):
        return 2 * ((chip + k // 2) % 2) + (core + k % 2) % 2

    def slot_y(k):
        return (jy + G - k) % G

    partners = [(None, at_x(p)) for p in xp] + [(None, at_y(p)) for p in yp]
    partners += [(None, at_y((gy + q) % G * G + jy)) for q in (1, 2, 3)]
    partners += [
        ((ix == 0) & (i > 0), at_x(i - 1)),
        ((ix == G - 1) & (i < NX_DEV - 1), at_x(i + 1)),
        (i >= G, at_x(i - G)),
        (i < NX_DEV - G, at_x(i + G)),
        ((jy == 0) & (j > 0), at_y(j - 1)),
        ((jy == G - 1) & (j < NY_DEV - 1), at_y(j + 1)),
    ]
    barrier = pltpu.get_barrier_semaphore()
    for held, where in partners:
        def greet(where=where):
            pl.semaphore_signal(barrier, inc=1, device_id=where, device_id_type=MESH)
        if held is None:
            greet()
        else:
            pl.when(held)(greet)
    edge_out[0] = start_ref[:, C - 1, :]
    edge_out[1] = start_ref[:, 0, :]
    count = 9
    for held, _ in partners[9:]:
        count = count + held.astype(jnp.int32)
    pl.semaphore_wait(barrier, count)

    def copy(src, dst, number, where):
        return pltpu.make_async_remote_copy(
            src_ref=src, dst_ref=dst, send_sem=send_sem.at[number],
            recv_sem=recv_sem.at[number], device_id=where, device_id_type=MESH,
        )

    halo = [
        (i < NX_DEV - 1, i > 0, copy(edge_out.at[0], edge_in.at[0], HALO, at_x(i + 1))),
        (i > 0, i < NX_DEV - 1, copy(edge_out.at[1], edge_in.at[1], HALO + 1, at_x(i - 1))),
        (j < NY_DEV - 1, j > 0,
         copy(start_ref.at[:, :, pl.ds(K // 2, K // 2)], row_in.at[0], HALO + 2, at_y(j + 1))),
        (j > 0, j < NY_DEV - 1,
         copy(start_ref.at[:, :, pl.ds(0, K // 2)], row_in.at[1], HALO + 3, at_y(j - 1))),
    ]
    for sends, _, move in halo:
        pl.when(sends)(move.start)

    ops_x = []
    for n, (ref, number) in enumerate(((fwd_x_ref, FX), (back_x_ref, BX))):
        ops_x.append([
            copy(ref, got_x.at[n, 0], number, at_x(xp[0])),
            copy(ref, got_x.at[n, 1], number + 1, at_x(xp[1])),
            copy(got_x.at[n, 1], got_x.at[n, 2], number + 2, at_x(xp[0])),
        ])
    ops_y = []
    for n, (ref, number) in enumerate(((fwd_y_ref, FY), (back_y_ref, BY))):
        ops_y.append([
            copy(ref, got_y.at[n, d], number + d, at_y(yp[d])) for d in range(3)
        ])
    fetches[0].wait()
    ops_x[0][1].start()
    ops_x[0][0].start()

    def widen(ref, target):
        high, low = split(ref[...])
        target[:, :K] = high
        target[:, K:] = low

    for move in fetches[1:]:
        move.wait()
    widen(couple_x_ref, wide_c.at[0])
    widen(couple_y_ref, wide_c.at[1])
    widen(fwd_x_ref, wide_x.at[0, 0])
    widen(back_x_ref, wide_x.at[1, 0])
    widen(fwd_y_ref, wide_y.at[0, 0])
    widen(back_y_ref, wide_y.at[1, 0])

    permit = jnp.zeros((C, K), jnp.float32)
    for c in range(8):
        permit = jnp.where(classes_ref[...] == c, perm_ref[c], permit)
    permit_ref[...] = permit

    lane = lax.broadcasted_iota(jnp.int32, (C, K), 1)
    col = lax.broadcasted_iota(jnp.int32, (C, K), 0)
    node = lane % Z
    mine = lane // Z == col

    for n, target in ((0, edge_in.at[0]), (1, edge_in.at[1]), (2, row_in.at[0]), (3, row_in.at[1])):
        _, receives, move = halo[n]
        pl.when(receives)(move.wait_recv)

        def clear(target=target):
            target[...] = jnp.zeros(target.shape, jnp.float32)
        pl.when(jnp.logical_not(receives))(clear)

    def by_four(body):
        def four(q, _):
            for r in range(4):
                body(4 * q + r, 0)
            return 0

        lax.fori_loop(0, E // 4, four, 0)

    def residual(e, _):
        x = start_ref[e]
        low = edge_in[0, pl.ds(e, 1), :]
        high = edge_in[1, pl.ds(e, 1), :]
        after = jnp.where(col == C - 1, high, pltpu.roll(x, C - 1, 0))
        before = jnp.where(col == 0, low, pltpu.roll(x, 1, 0))
        piece = row_in[0, e]
        row_before = pltpu.roll(
            jnp.where(lane >= K - Z, jnp.concatenate([piece, piece], axis=1), x), Z, 1)
        piece = row_in[1, e]
        row_after = pltpu.roll(
            jnp.where(lane < Z, jnp.concatenate([piece, piece], axis=1), x), K - Z, 1)
        beside = after + before + row_after + row_before
        upper = jnp.where(node == Z - 1, 0.0, pltpu.roll(x, K - 1, 1))
        lower = jnp.where(node == 0, 0.0, pltpu.roll(x, 1, 1))
        source = jnp.where(conductor_ref[...] == e, drive_ref[...], 0.0)
        resid = source - (permit_ref[...] * (4.0 * x - beside) + 2.0 * x - (upper + lower))
        resid_ref[e] = resid
        src_ref[0, 0, pl.ds(e, 1), :] = jnp.sum(leaf_x_ref[...] * resid, axis=0, keepdims=True)
        return 0

    by_four(residual)

    def share(n, number, places):
        moves = [
            copy(src_ref.at[n, 0], src_ref.at[n, d + 1], number + d, places[d])
            for d in range(3)
        ]
        for move in reversed(moves):
            move.start()
        return moves

    def compose(n, wide, way, slot, order, position):
        def part(h, _):
            rows = pl.ds(pl.multiple_of(h * ROWS, ROWS), ROWS)

            def put(target, x):
                high, low = split(x * DOWN)
                target[n, rows, :K] = high
                target[n, rows, K:] = low

            pair = wide[way, slot(order[0]), rows, :]
            high, low = pair[:, :K], pair[:, K:]
            x = high.astype(jnp.float32) + low.astype(jnp.float32)
            pl.when(position == order[0])(functools.partial(put, prefix_ref, x))
            for k in order[1:]:
                x = product_of(high, low, wide[way, slot(k)])
                pl.when(position == k)(functools.partial(put, prefix_ref, x))
                high, low = split(x)
            put(whole_ref, x)
            if n >= 2:
                whole_out[n - 2, rows, :] = x * DOWN
            return 0

        lax.fori_loop(0, K // ROWS, part, 0)

    def step_of(n, number, to):
        return copy(state_out.at[n], state_in.at[n], number, to)

    def inside(n, moves, wide, way, slot, order, position, first=None, step=None):
        for move in moves:
            move.wait_recv()
        state = src_ref[n, slot(order[0])] * DOWN
        kept = state
        for k in order[1:]:
            s = slot(k)
            state = product(state, wide[way, s]) + src_ref[n, s] * DOWN
            kept = jnp.where(position == k, state, kept)
        kept_ref[n] = kept
        if step is None:
            state_out[n] = state
            for a, _, move in tails[n - 2]:
                pl.when(rank[n - 2] == a)(move.start)
            return
        tail_ref[n] = state

        def begin():
            state_out[n] = state * UP
            step.start()
            state_in[n] = jnp.zeros((E, K), jnp.float32)
        pl.when(first)(begin)

    def across_groups(n, first, last, step):
        def take():
            step.wait_recv()
        pl.when(jnp.logical_not(first))(take)

        def give():
            state_out[n] = (product(state_in[n], whole_ref[n]) + tail_ref[n]) * UP
            step.start()
        pl.when(jnp.logical_not(first) & jnp.logical_not(last))(give)
        return (product(state_in[n], prefix_ref[n]) + kept_ref[n]) * UP

    def entry_y(n):
        state_in[n] = jnp.zeros((E, K), jnp.float32)
        for place in range(3):
            def take(place=place):
                for a, b, move in tails[n - 2]:
                    if a == place:
                        pl.when(rank[n - 2] == b)(move.wait_recv)
                state = tails_in[n - 2, place]
                if place:
                    state = product(state_in[n], wide_in[n - 2, place - 1]) + state
                state_in[n] = state * UP
            pl.when(rank[n - 2] > place)(take)
        return (product(state_in[n], prefix_ref[n]) + kept_ref[n]) * UP

    rank = (gy, G - 1 - gy)

    def member(way, place):
        return at_y((place if way == 0 else G - 1 - place) * G + jy)

    wholes = [
        [(a, b, copy(whole_out.at[n], whole_in.at[n, a - 1], WY + 3 * n + q, member(n, b)))
         for q, (a, b) in enumerate(WHOLE_PAIRS)]
        for n in range(2)
    ]
    tails = [
        [(a, b, copy(state_out.at[2 + n], tails_in.at[n, a], TY + 6 * n + q, member(n, b)))
         for q, (a, b) in enumerate(TAIL_PAIRS)]
        for n in range(2)
    ]
    up, down = (0, 1, 2, 3), (3, 2, 1, 0)
    x_first, x_last = i < G, i >= NX_DEV - G
    step_xf = step_of(0, EXF, at_x(i + G))
    step_xb = step_of(1, EXB, at_x(i - G))
    early = i < NX_DEV // 2
    late = jnp.logical_not(early)
    before = i < NX_DEV - 2 * G

    def receive_x(n):
        ops_x[n][1].wait_recv()
        ops_x[n][2].start()
        widen(got_x.at[n, 1], wide_x.at[n, 2])
        ops_x[n][0].wait_recv()
        widen(got_x.at[n, 0], wide_x.at[n, 1])
        ops_x[n][2].wait_recv()
        widen(got_x.at[n, 2], wide_x.at[n, 3])

    def ready_back_x():
        receive_x(1)
        compose(1, wide_x, 1, slot_x, down, ix)

    def ready_y():
        for n, order in ((0, up), (1, down)):
            for d in range(3):
                ops_y[n][d].wait_recv()
                widen(got_y.at[n, d], wide_y.at[n, d + 1])
            compose(2 + n, wide_y, n, slot_y, order, jy)
            for a, _, move in wholes[n]:
                pl.when(rank[n] == a)(move.start)
        for n in range(2):
            for a, b, move in wholes[n]:
                def take(a=a, move=move, n=n):
                    move.wait_recv()
                    widen(whole_in.at[n, a - 1], wide_in.at[n, a - 1])
                pl.when(rank[n] == b)(take)

    moves_sx = share(0, SX, [at_x(p) for p in xp])
    receive_x(0)
    inside(0, moves_sx, wide_x, 0, slot_x, up, ix, x_first, step_xf)
    ops_x[1][1].start()
    ops_x[1][0].start()
    for n in range(2):
        for move in ops_y[n]:
            move.start()
    compose(0, wide_x, 0, slot_x, up, ix)
    pl.when(late)(ready_back_x)
    ahead = across_groups(0, x_first, x_last, step_xf)
    src_ref[1, 0] = product(ahead, wide_c[0])
    moves_qx = share(1, QX, [at_x(p) for p in xp])
    pl.when(early)(ready_back_x)
    inside(1, moves_qx, wide_x, 1, slot_x, down, ix, x_last, step_xb)
    pl.when(before)(ready_y)
    across_ref[...] = across_groups(1, x_last, x_first, step_xb)

    def gather_y(e, _):
        lifted = resid_ref[e] + leaf_x_ref[...] * across_ref[pl.ds(e, 1), :]
        t = lifted * leaf_y_ref[...]
        for shift in (128, 64, 32, 16):
            t = t + pltpu.roll(t, shift, 1)
        src_ref[2, 0, pl.ds(e, 1), :] = jnp.sum(jnp.where(mine, t, 0.0), axis=0, keepdims=True)
        return 0

    by_four(gather_y)
    moves_sy = share(2, SY, [at_y(p) for p in yp])
    pl.when(jnp.logical_not(before))(ready_y)
    inside(2, moves_sy, wide_y, 0, slot_y, up, jy)
    ahead = entry_y(2)
    src_ref[3, 0] = product(ahead, wide_c[1])
    moves_qy = share(3, QY, [at_y(p) for p in yp])
    inside(3, moves_qy, wide_y, 1, slot_y, down, jy)
    along_ref[...] = entry_y(3)

    def finish(e, _):
        t = jnp.where(mine, along_ref[pl.ds(e, 1), :], 0.0)
        for shift in (128, 64, 32, 16):
            t = t + pltpu.roll(t, shift, 1)
        out_ref[e] = (
            start_ref[e] + leaf_x_ref[...] * across_ref[pl.ds(e, 1), :] + leaf_y_ref[...] * t
        )
        return 0

    by_four(finish)

    for sends, _, move in halo:
        pl.when(sends)(move.wait_send)
    for moves in ops_x + ops_y + [moves_sx, moves_qx, moves_sy, moves_qy]:
        for move in moves:
            move.wait_send()
    pl.when(jnp.logical_not(x_last))(step_xf.wait_send)
    pl.when(jnp.logical_not(x_first))(step_xb.wait_send)
    for n in range(2):
        for a, _, move in wholes[n] + tails[n]:
            pl.when(rank[n] == a)(move.wait_send)


def local(*arrays):
    vmem = pl.BlockSpec(memory_space=pltpu.VMEM)
    smem = pl.BlockSpec(memory_space=pltpu.SMEM)
    hbm = pl.BlockSpec(memory_space=pl.ANY)
    f32, bf16 = jnp.float32, jnp.bfloat16
    return pl.pallas_call(
        kernel,
        out_shape=jax.ShapeDtypeStruct((E, C, K), f32),
        in_specs=[vmem] * 4 + [smem] + [vmem] * 2 + [hbm] * 6,
        out_specs=vmem,
        scratch_shapes=[
            pltpu.VMEM((6, K, K), f32),
            pltpu.VMEM((2, E, K), f32),
            pltpu.VMEM((2, E, K), f32),
            pltpu.VMEM((2, E, C, K // 2), f32),
            pltpu.VMEM((E, C, K), f32),
            pltpu.VMEM((C, K), f32),
            pltpu.VMEM((2, 3, K, K), f32),
            pltpu.VMEM((2, 3, K, K), f32),
            pltpu.VMEM((2, G, K, 2 * K), bf16),
            pltpu.VMEM((2, G, K, 2 * K), bf16),
            pltpu.VMEM((2, K, 2 * K), bf16),
            pltpu.VMEM((4, K, 2 * K), bf16),
            pltpu.VMEM((4, K, 2 * K), bf16),
            pltpu.VMEM((2, K, K), f32),
            pltpu.VMEM((2, 2, K, K), f32),
            pltpu.VMEM((2, 2, K, 2 * K), bf16),
            pltpu.VMEM((4, G, E, K), f32),
            pltpu.VMEM((4, E, K), f32),
            pltpu.VMEM((4, E, K), f32),
            pltpu.VMEM((4, E, K), f32),
            pltpu.VMEM((4, E, K), f32),
            pltpu.VMEM((2, 3, E, K), f32),
            pltpu.VMEM((E, K), f32),
            pltpu.VMEM((E, K), f32),
            pltpu.SemaphoreType.DMA((COPIES,)),
            pltpu.SemaphoreType.DMA((COPIES,)),
            pltpu.SemaphoreType.DMA((6,)),
        ],
        compiler_params=pltpu.CompilerParams(
            collective_id=0, has_side_effects=True, vmem_limit_bytes=48 * 1024 * 1024
        ),
    )(*arrays)


def solution(mesh):
    split_two = P("gx", "gy")
    in_specs = (P(None, "gx", "gy"),) + (split_two,) * 3 + (P(),) + (split_two,) * 8
    return jax.shard_map(
        local, mesh=mesh, in_specs=in_specs, out_specs=P(None, "gx", "gy"), check_vma=False
    )
```

```python
import functools

import jax
import jax.numpy as jnp
from jax import lax
from jax.experimental import pallas as pl
from jax.experimental.pallas import tpu as pltpu
from jax.sharding import PartitionSpec as P

Z = 16
E = 16
C = 16
K = 256
NX_DEV = 32
NY_DEV = 16
G = 4
MESH = pl.DeviceIdType.MESH

HALO = 0
FX, BX, FY, BY = 4, 7, 10, 13
SX, QX, SY, QY = 16, 19, 22, 25
EXF, EXB = 28, 29
WY = 30
TY = 36
EXB_NEAR, TX, WX = 48, 49, 50
COPIES = 51
WHOLE_PAIRS = ((1, 2), (1, 3), (2, 3))
TAIL_PAIRS = ((0, 1), (0, 2), (0, 3), (1, 2), (1, 3), (2, 3))

DOWN, UP = 2.0**-24, 2.0**24
ROWS = 128


def split(x):
    high = x.astype(jnp.bfloat16)
    low = (x - high.astype(jnp.float32)).astype(jnp.bfloat16)
    return high, low


def product_of(high, low, wide):
    rows = high.shape[0]
    r = jnp.dot(
        jnp.concatenate([high, low], axis=0), wide, preferred_element_type=jnp.float32
    )
    return (r[rows:, K:] + r[:rows, K:] + r[rows:, :K]) + r[:rows, :K]


def product(state, wide):
    return product_of(*split(state), wide)


def kernel(
    start_ref, classes_ref, conductor_ref, drive_ref, perm_ref, leaf_x_ref, leaf_y_ref,
    fwd_x_hbm, back_x_hbm, couple_x_hbm, fwd_y_hbm, back_y_hbm, couple_y_hbm,
    out_ref,
    own_ref, tail_x_in, wide_x_in,
    edge_out, edge_in, row_in, resid_ref, permit_ref,
    got_x, got_y, wide_x, wide_y, wide_c, whole_ref, prefix_ref, whole_out, whole_in, wide_in,
    src_ref, kept_ref, tail_ref, state_out, state_in, tails_in, across_ref, along_ref,
    send_sem, recv_sem, own_sem,
):
    fetches = [
        pltpu.make_async_copy(ref, own_ref.at[n], own_sem.at[n])
        for n, ref in enumerate(
            (fwd_x_hbm, couple_x_hbm, couple_y_hbm, back_x_hbm, fwd_y_hbm, back_y_hbm))
    ]
    for move in fetches:
        move.start()
    fwd_x_ref, couple_x_ref, couple_y_ref, back_x_ref, fwd_y_ref, back_y_ref = (
        own_ref.at[n] for n in range(6))
    i = lax.axis_index("gx")
    j = lax.axis_index("gy")
    ix, gx = i % G, i // G
    jy, gy = j % G, j // G
    core, chip = ix % 2, ix // 2

    def at_x(index):
        return (index, j)

    def at_y(index):
        return (i, index)

    xp = [
        gx * G + 2 * chip + (1 - core),
        gx * G + 2 * (1 - chip) + core,
        gx * G + 2 * (1 - chip) + (1 - core),
    ]
    yp = [gy * G + (jy + d) % G for d in (1, 2, 3)]

    def slot_x(k):
        return 2 * ((chip + k // 2) % 2) + (core + k % 2) % 2

    def slot_y(k):
        return (jy + G - k) % G

    partners = [(None, at_x(p)) for p in xp] + [(None, at_y(p)) for p in yp]
    partners += [(None, at_y((gy + q) % G * G + jy)) for q in (1, 2, 3)]
    partners += [
        ((ix == 0) & (i > 0), at_x(i - 1)),
        ((ix == G - 1) & (i < NX_DEV - 1), at_x(i + 1)),
        (i >= G, at_x(i - G)),
        (i < NX_DEV - G, at_x(i + G)),
        ((gx % 2 == 0) & (gx >= 2), at_x(i - 2 * G)),
        ((gx % 2 == 0) & (gx <= 4), at_x(i + 2 * G)),
        ((jy == 0) & (j > 0), at_y(j - 1)),
        ((jy == G - 1) & (j < NY_DEV - 1), at_y(j + 1)),
    ]
    barrier = pltpu.get_barrier_semaphore()
    for held, where in partners:
        def greet(where=where):
            pl.semaphore_signal(barrier, inc=1, device_id=where, device_id_type=MESH)
        if held is None:
            greet()
        else:
            pl.when(held)(greet)
    edge_out[0] = start_ref[:, C - 1, :]
    edge_out[1] = start_ref[:, 0, :]
    count = 9
    for held, _ in partners[9:]:
        count = count + held.astype(jnp.int32)
    pl.semaphore_wait(barrier, count)

    def copy(src, dst, number, where):
        return pltpu.make_async_remote_copy(
            src_ref=src, dst_ref=dst, send_sem=send_sem.at[number],
            recv_sem=recv_sem.at[number], device_id=where, device_id_type=MESH,
        )

    halo = [
        (i < NX_DEV - 1, i > 0, copy(edge_out.at[0], edge_in.at[0], HALO, at_x(i + 1))),
        (i > 0, i < NX_DEV - 1, copy(edge_out.at[1], edge_in.at[1], HALO + 1, at_x(i - 1))),
        (j < NY_DEV - 1, j > 0,
         copy(start_ref.at[:, :, pl.ds(K // 2, K // 2)], row_in.at[0], HALO + 2, at_y(j + 1))),
        (j > 0, j < NY_DEV - 1,
         copy(start_ref.at[:, :, pl.ds(0, K // 2)], row_in.at[1], HALO + 3, at_y(j - 1))),
    ]
    for sends, _, move in halo:
        pl.when(sends)(move.start)

    ops_x = []
    for n, (ref, number) in enumerate(((fwd_x_ref, FX), (back_x_ref, BX))):
        ops_x.append([
            copy(ref, got_x.at[n, 0], number, at_x(xp[0])),
            copy(ref, got_x.at[n, 1], number + 1, at_x(xp[1])),
            copy(got_x.at[n, 1], got_x.at[n, 2], number + 2, at_x(xp[0])),
        ])
    ops_y = []
    for n, (ref, number) in enumerate(((fwd_y_ref, FY), (back_y_ref, BY))):
        ops_y.append([
            copy(ref, got_y.at[n, d], number + d, at_y(yp[d])) for d in range(3)
        ])
    fetches[0].wait()
    ops_x[0][1].start()
    ops_x[0][0].start()

    def widen(ref, target):
        high, low = split(ref[...])
        target[:, :K] = high
        target[:, K:] = low

    for move in fetches[1:]:
        move.wait()
    widen(couple_x_ref, wide_c.at[0])
    widen(couple_y_ref, wide_c.at[1])
    widen(fwd_x_ref, wide_x.at[0, 0])
    widen(back_x_ref, wide_x.at[1, 0])
    widen(fwd_y_ref, wide_y.at[0, 0])
    widen(back_y_ref, wide_y.at[1, 0])

    permit = jnp.zeros((C, K), jnp.float32)
    for c in range(8):
        permit = jnp.where(classes_ref[...] == c, perm_ref[c], permit)
    permit_ref[...] = permit

    lane = lax.broadcasted_iota(jnp.int32, (C, K), 1)
    col = lax.broadcasted_iota(jnp.int32, (C, K), 0)
    node = lane % Z
    mine = lane // Z == col

    for n, target in ((0, edge_in.at[0]), (1, edge_in.at[1]), (2, row_in.at[0]), (3, row_in.at[1])):
        _, receives, move = halo[n]
        pl.when(receives)(move.wait_recv)

        def clear(target=target):
            target[...] = jnp.zeros(target.shape, jnp.float32)
        pl.when(jnp.logical_not(receives))(clear)

    def by_four(body):
        def four(q, _):
            for r in range(4):
                body(4 * q + r, 0)
            return 0

        lax.fori_loop(0, E // 4, four, 0)

    def residual(e, _):
        x = start_ref[e]
        low = edge_in[0, pl.ds(e, 1), :]
        high = edge_in[1, pl.ds(e, 1), :]
        after = jnp.where(col == C - 1, high, pltpu.roll(x, C - 1, 0))
        before = jnp.where(col == 0, low, pltpu.roll(x, 1, 0))
        piece = row_in[0, e]
        row_before = pltpu.roll(
            jnp.where(lane >= K - Z, jnp.concatenate([piece, piece], axis=1), x), Z, 1)
        piece = row_in[1, e]
        row_after = pltpu.roll(
            jnp.where(lane < Z, jnp.concatenate([piece, piece], axis=1), x), K - Z, 1)
        beside = after + before + row_after + row_before
        upper = jnp.where(node == Z - 1, 0.0, pltpu.roll(x, K - 1, 1))
        lower = jnp.where(node == 0, 0.0, pltpu.roll(x, 1, 1))
        source = jnp.where(conductor_ref[...] == e, drive_ref[...], 0.0)
        resid = source - (permit_ref[...] * (4.0 * x - beside) + 2.0 * x - (upper + lower))
        resid_ref[e] = resid
        src_ref[0, 0, pl.ds(e, 1), :] = jnp.sum(leaf_x_ref[...] * resid, axis=0, keepdims=True)
        return 0

    by_four(residual)

    def share(n, number, places):
        moves = [
            copy(src_ref.at[n, 0], src_ref.at[n, d + 1], number + d, places[d])
            for d in range(3)
        ]
        for move in reversed(moves):
            move.start()
        return moves

    def compose(n, wide, way, slot, order, position):
        def part(h, _):
            rows = pl.ds(pl.multiple_of(h * ROWS, ROWS), ROWS)

            def put(target, x):
                high, low = split(x * DOWN)
                target[n, rows, :K] = high
                target[n, rows, K:] = low

            pair = wide[way, slot(order[0]), rows, :]
            high, low = pair[:, :K], pair[:, K:]
            x = high.astype(jnp.float32) + low.astype(jnp.float32)
            pl.when(position == order[0])(functools.partial(put, prefix_ref, x))
            for k in order[1:]:
                x = product_of(high, low, wide[way, slot(k)])
                pl.when(position == k)(functools.partial(put, prefix_ref, x))
                high, low = split(x)
            put(whole_ref, x)
            if n >= 1:
                whole_out[(n + 1) % 3, rows, :] = x * DOWN
            return 0

        lax.fori_loop(0, K // ROWS, part, 0)

    def step_of(n, number, to):
        return copy(state_out.at[n], state_in.at[n], number, to)

    def inside(n, moves, wide, way, slot, order, position, first=None, step=None):
        for move in moves:
            move.wait_recv()
        state = src_ref[n, slot(order[0])] * DOWN
        kept = state
        for k in order[1:]:
            s = slot(k)
            state = product(state, wide[way, s]) + src_ref[n, s] * DOWN
            kept = jnp.where(position == k, state, kept)
        kept_ref[n] = kept
        if n == 1:
            tail_ref[n] = state

            def pass_tail():
                state_out[n] = state
                tail_x.start()
            pl.when(odd)(pass_tail)

            def clear():
                state_in[n] = jnp.zeros((E, K), jnp.float32)
            pl.when(gx >= 6)(clear)
            return
        if step is None:
            state_out[n] = state
            for a, _, move in tails[n - 2]:
                pl.when(rank[n - 2] == a)(move.start)
            return
        tail_ref[n] = state

        def begin():
            state_out[n] = state * UP
            step.start()
            state_in[n] = jnp.zeros((E, K), jnp.float32)
        pl.when(first)(begin)

    def across_groups(n, first, last, step):
        def take():
            step.wait_recv()
        pl.when(jnp.logical_not(first))(take)

        def give():
            state_out[n] = (product(state_in[n], whole_ref[n]) + tail_ref[n]) * UP
            step.start()
        pl.when(jnp.logical_not(first) & jnp.logical_not(last))(give)
        return (product(state_in[n], prefix_ref[n]) + kept_ref[n]) * UP

    def entry_y(n):
        state_in[n] = jnp.zeros((E, K), jnp.float32)
        for place in range(3):
            def take(place=place):
                for a, b, move in tails[n - 2]:
                    if a == place:
                        pl.when(rank[n - 2] == b)(move.wait_recv)
                state = tails_in[n - 2, place]
                if place:
                    state = product(state_in[n], wide_in[n - 2, place - 1]) + state
                state_in[n] = state * UP
            pl.when(rank[n - 2] > place)(take)
        return (product(state_in[n], prefix_ref[n]) + kept_ref[n]) * UP

    rank = (gy, G - 1 - gy)

    def member(way, place):
        return at_y((place if way == 0 else G - 1 - place) * G + jy)

    wholes = [
        [(a, b, copy(whole_out.at[n], whole_in.at[n, a - 1], WY + 3 * n + q, member(n, b)))
         for q, (a, b) in enumerate(WHOLE_PAIRS)]
        for n in range(2)
    ]
    tails = [
        [(a, b, copy(state_out.at[2 + n], tails_in.at[n, a], TY + 6 * n + q, member(n, b)))
         for q, (a, b) in enumerate(TAIL_PAIRS)]
        for n in range(2)
    ]
    up, down = (0, 1, 2, 3), (3, 2, 1, 0)
    x_first, x_last = i < G, i >= NX_DEV - G
    step_xf = step_of(0, EXF, at_x(i + G))
    odd = gx % 2 == 1
    even = jnp.logical_not(odd)
    far = step_of(1, EXB, at_x(i - 2 * G))
    near = step_of(1, EXB_NEAR, at_x(i - G))
    tail_x = copy(state_out.at[1], tail_x_in, TX, at_x(i - G))
    whole_x = copy(whole_out.at[2], whole_in.at[2, 0], WX, at_x(i - G))

    def entry_back_x():
        pl.when(odd & (gx < 6))(near.wait_recv)

        def pair():
            pl.when(gx < 6)(far.wait_recv)
            tail_x.wait_recv()

            def through():
                state_in[1] = (product(state_in[1], wide_x_in[...]) + tail_x_in[...]) * UP
            pl.when(gx < 6)(through)

            def only():
                state_in[1] = tail_x_in[...] * UP
            pl.when(gx >= 6)(only)

            def give():
                state_out[1] = (product(state_in[1], whole_ref[1]) + tail_ref[1]) * UP
                far.start()
                near.start()
            pl.when(gx >= 2)(give)
        pl.when(even)(pair)
        return (product(state_in[1], prefix_ref[1]) + kept_ref[1]) * UP

    early = i < NX_DEV // 2
    late = jnp.logical_not(early)
    before = i < NX_DEV - 2 * G

    def receive_x(n):
        ops_x[n][1].wait_recv()
        ops_x[n][2].start()
        widen(got_x.at[n, 1], wide_x.at[n, 2])
        ops_x[n][0].wait_recv()
        widen(got_x.at[n, 0], wide_x.at[n, 1])
        ops_x[n][2].wait_recv()
        widen(got_x.at[n, 2], wide_x.at[n, 3])

    def ready_back_x():
        receive_x(1)
        compose(1, wide_x, 1, slot_x, down, ix)
        pl.when(odd & (gx < 6))(whole_x.start)

    def ready_y():
        for n, order in ((0, up), (1, down)):
            for d in range(3):
                ops_y[n][d].wait_recv()
                widen(got_y.at[n, d], wide_y.at[n, d + 1])
            compose(2 + n, wide_y, n, slot_y, order, jy)
            for a, _, move in wholes[n]:
                pl.when(rank[n] == a)(move.start)
        for n in range(2):
            for a, b, move in wholes[n]:
                def take(a=a, move=move, n=n):
                    move.wait_recv()
                    widen(whole_in.at[n, a - 1], wide_in.at[n, a - 1])
                pl.when(rank[n] == b)(take)

    moves_sx = share(0, SX, [at_x(p) for p in xp])
    receive_x(0)
    inside(0, moves_sx, wide_x, 0, slot_x, up, ix, x_first, step_xf)
    ops_x[1][1].start()
    ops_x[1][0].start()
    for n in range(2):
        for move in ops_y[n]:
            move.start()
    compose(0, wide_x, 0, slot_x, up, ix)
    pl.when(late)(ready_back_x)
    ahead = across_groups(0, x_first, x_last, step_xf)
    src_ref[1, 0] = product(ahead, wide_c[0])
    moves_qx = share(1, QX, [at_x(p) for p in xp])
    pl.when(early)(ready_back_x)
    inside(1, moves_qx, wide_x, 1, slot_x, down, ix)

    def take_whole_x():
        whole_x.wait_recv()
        widen(whole_in.at[2, 0], wide_x_in)
    pl.when(even & (gx < 6))(take_whole_x)
    pl.when(before)(ready_y)
    across_ref[...] = entry_back_x()

    def gather_y(e, _):
        lifted = resid_ref[e] + leaf_x_ref[...] * across_ref[pl.ds(e, 1), :]
        t = lifted * leaf_y_ref[...]
        for shift in (128, 64, 32, 16):
            t = t + pltpu.roll(t, shift, 1)
        src_ref[2, 0, pl.ds(e, 1), :] = jnp.sum(jnp.where(mine, t, 0.0), axis=0, keepdims=True)
        return 0

    by_four(gather_y)
    moves_sy = share(2, SY, [at_y(p) for p in yp])
    pl.when(jnp.logical_not(before))(ready_y)
    inside(2, moves_sy, wide_y, 0, slot_y, up, jy)
    ahead = entry_y(2)
    src_ref[3, 0] = product(ahead, wide_c[1])
    moves_qy = share(3, QY, [at_y(p) for p in yp])
    inside(3, moves_qy, wide_y, 1, slot_y, down, jy)
    along_ref[...] = entry_y(3)

    def finish(e, _):
        t = jnp.where(mine, along_ref[pl.ds(e, 1), :], 0.0)
        for shift in (128, 64, 32, 16):
            t = t + pltpu.roll(t, shift, 1)
        out_ref[e] = (
            start_ref[e] + leaf_x_ref[...] * across_ref[pl.ds(e, 1), :] + leaf_y_ref[...] * t
        )
        return 0

    by_four(finish)

    for sends, _, move in halo:
        pl.when(sends)(move.wait_send)
    for moves in ops_x + ops_y + [moves_sx, moves_qx, moves_sy, moves_qy]:
        for move in moves:
            move.wait_send()
    pl.when(jnp.logical_not(x_last))(step_xf.wait_send)
    for move in (far, near):
        pl.when(even & (gx >= 2))(move.wait_send)
    pl.when(odd)(tail_x.wait_send)
    pl.when(odd & (gx < 6))(whole_x.wait_send)
    for n in range(2):
        for a, _, move in wholes[n] + tails[n]:
            pl.when(rank[n] == a)(move.wait_send)


def local(*arrays):
    vmem = pl.BlockSpec(memory_space=pltpu.VMEM)
    smem = pl.BlockSpec(memory_space=pltpu.SMEM)
    hbm = pl.BlockSpec(memory_space=pl.ANY)
    f32, bf16 = jnp.float32, jnp.bfloat16
    return pl.pallas_call(
        kernel,
        out_shape=jax.ShapeDtypeStruct((E, C, K), f32),
        in_specs=[vmem] * 4 + [smem] + [vmem] * 2 + [hbm] * 6,
        out_specs=vmem,
        scratch_shapes=[
            pltpu.VMEM((6, K, K), f32),
            pltpu.VMEM((E, K), f32),
            pltpu.VMEM((K, 2 * K), bf16),
            pltpu.VMEM((2, E, K), f32),
            pltpu.VMEM((2, E, K), f32),
            pltpu.VMEM((2, E, C, K // 2), f32),
            pltpu.VMEM((E, C, K), f32),
            pltpu.VMEM((C, K), f32),
            pltpu.VMEM((2, 3, K, K), f32),
            pltpu.VMEM((2, 3, K, K), f32),
            pltpu.VMEM((2, G, K, 2 * K), bf16),
            pltpu.VMEM((2, G, K, 2 * K), bf16),
            pltpu.VMEM((2, K, 2 * K), bf16),
            pltpu.VMEM((4, K, 2 * K), bf16),
            pltpu.VMEM((4, K, 2 * K), bf16),
            pltpu.VMEM((3, K, K), f32),
            pltpu.VMEM((3, 2, K, K), f32),
            pltpu.VMEM((2, 2, K, 2 * K), bf16),
            pltpu.VMEM((4, G, E, K), f32),
            pltpu.VMEM((4, E, K), f32),
            pltpu.VMEM((4, E, K), f32),
            pltpu.VMEM((4, E, K), f32),
            pltpu.VMEM((4, E, K), f32),
            pltpu.VMEM((2, 3, E, K), f32),
            pltpu.VMEM((E, K), f32),
            pltpu.VMEM((E, K), f32),
            pltpu.SemaphoreType.DMA((COPIES,)),
            pltpu.SemaphoreType.DMA((COPIES,)),
            pltpu.SemaphoreType.DMA((6,)),
        ],
        compiler_params=pltpu.CompilerParams(
            collective_id=0, has_side_effects=True, vmem_limit_bytes=63 * 1024 * 1024
        ),
    )(*arrays)


def solution(mesh):
    split_two = P("gx", "gy")
    in_specs = (P(None, "gx", "gy"),) + (split_two,) * 3 + (P(),) + (split_two,) * 8
    return jax.shard_map(
        local, mesh=mesh, in_specs=in_specs, out_specs=P(None, "gx", "gy"), check_vma=False
    )
```

```python
import functools

import jax
import jax.numpy as jnp
from jax import lax
from jax.experimental import pallas as pl
from jax.experimental.pallas import tpu as pltpu
from jax.sharding import PartitionSpec as P

Z = 16
E = 16
C = 16
K = 256
NX_DEV = 32
NY_DEV = 16
G = 4
MESH = pl.DeviceIdType.MESH

HALO = 0
FX, BX, FY, BY = 4, 7, 10, 13
SX, QX, SY, QY = 16, 19, 22, 25
EXF, EXB = 28, 29
WY = 30
TY = 36
EXB_NEAR, TX, WX = 48, 49, 50
EXF_FAR, TXF, WXF = 51, 52, 53
COPIES = 54
WHOLE_PAIRS = ((1, 2), (1, 3), (2, 3))
TAIL_PAIRS = ((0, 1), (0, 2), (0, 3), (1, 2), (1, 3), (2, 3))

DOWN, UP = 2.0**-24, 2.0**24
ROWS = 128


def split(x):
    high = x.astype(jnp.bfloat16)
    low = (x - high.astype(jnp.float32)).astype(jnp.bfloat16)
    return high, low


def product_of(high, low, wide):
    rows = high.shape[0]
    r = jnp.dot(
        jnp.concatenate([high, low], axis=0), wide, preferred_element_type=jnp.float32
    )
    return (r[rows:, K:] + r[:rows, K:] + r[rows:, :K]) + r[:rows, :K]


def product(state, wide):
    return product_of(*split(state), wide)


def kernel(
    start_hbm, classes_hbm, conductor_hbm, drive_hbm, perm_ref, leaf_x_hbm, leaf_y_hbm,
    fwd_x_hbm, back_x_hbm, couple_x_hbm, fwd_y_hbm, back_y_hbm, couple_y_hbm,
    out_ref,
    own_ref, tail_x_in, wide_x_in, tail_f_in, wide_f_in,
    start_ref, classes_ref, conductor_ref, drive_ref, leaf_x_ref, leaf_y_ref,
    edge_out, edge_in, row_in, resid_ref, permit_ref,
    got_x, got_y, wide_x, wide_y, wide_c, whole_ref, prefix_ref, whole_out, whole_in, wide_in,
    src_ref, kept_ref, tail_ref, state_out, state_in, tails_in, across_ref, along_ref,
    send_sem, recv_sem, own_sem,
):
    fetches = [
        pltpu.make_async_copy(ref, own_ref.at[n], own_sem.at[n])
        for n, ref in enumerate(
            (fwd_x_hbm, couple_x_hbm, couple_y_hbm, back_x_hbm, fwd_y_hbm, back_y_hbm))
    ]
    cells = [
        pltpu.make_async_copy(src, dst, own_sem.at[6 + n])
        for n, (src, dst) in enumerate((
            (start_hbm, start_ref), (classes_hbm, classes_ref), (conductor_hbm, conductor_ref),
            (drive_hbm, drive_ref), (leaf_x_hbm, leaf_x_ref), (leaf_y_hbm, leaf_y_ref)))
    ]
    fwd_x_ref, couple_x_ref, couple_y_ref, back_x_ref, fwd_y_ref, back_y_ref = (
        own_ref.at[n] for n in range(6))
    i = lax.axis_index("gx")
    j = lax.axis_index("gy")
    ix, gx = i % G, i // G
    jy, gy = j % G, j // G
    core, chip = ix % 2, ix // 2

    def at_x(index):
        return (index, j)

    def at_y(index):
        return (i, index)

    xp = [
        gx * G + 2 * chip + (1 - core),
        gx * G + 2 * (1 - chip) + core,
        gx * G + 2 * (1 - chip) + (1 - core),
    ]
    yp = [gy * G + (jy + d) % G for d in (1, 2, 3)]

    def slot_x(k):
        return 2 * ((chip + k // 2) % 2) + (core + k % 2) % 2

    def slot_y(k):
        return (jy + G - k) % G

    partners = [(None, at_x(p)) for p in xp] + [(None, at_y(p)) for p in yp]
    partners += [(None, at_y((gy + q) % G * G + jy)) for q in (1, 2, 3)]
    partners += [
        ((ix == 0) & (i > 0), at_x(i - 1)),
        ((ix == G - 1) & (i < NX_DEV - 1), at_x(i + 1)),
        (i >= G, at_x(i - G)),
        (i < NX_DEV - G, at_x(i + G)),
        (((gx % 2 == 0) & (gx >= 2)) | (gx == 5) | (gx == 7), at_x(i - 2 * G)),
        (((gx % 2 == 0) & (gx <= 4)) | (gx == 3) | (gx == 5), at_x(i + 2 * G)),
        ((jy == 0) & (j > 0), at_y(j - 1)),
        ((jy == G - 1) & (j < NY_DEV - 1), at_y(j + 1)),
    ]
    barrier = pltpu.get_barrier_semaphore()
    for held, where in partners:
        def greet(where=where):
            pl.semaphore_signal(barrier, inc=1, device_id=where, device_id_type=MESH)
        if held is None:
            greet()
        else:
            pl.when(held)(greet)
    for move in cells + fetches:
        move.start()
    cells[0].wait()
    edge_out[0] = start_ref[:, C - 1, :]
    edge_out[1] = start_ref[:, 0, :]
    count = 9
    for held, _ in partners[9:]:
        count = count + held.astype(jnp.int32)
    pl.semaphore_wait(barrier, count)

    def copy(src, dst, number, where):
        return pltpu.make_async_remote_copy(
            src_ref=src, dst_ref=dst, send_sem=send_sem.at[number],
            recv_sem=recv_sem.at[number], device_id=where, device_id_type=MESH,
        )

    halo = [
        (i < NX_DEV - 1, i > 0, copy(edge_out.at[0], edge_in.at[0], HALO, at_x(i + 1))),
        (i > 0, i < NX_DEV - 1, copy(edge_out.at[1], edge_in.at[1], HALO + 1, at_x(i - 1))),
        (j < NY_DEV - 1, j > 0,
         copy(start_ref.at[:, :, pl.ds(K // 2, K // 2)], row_in.at[0], HALO + 2, at_y(j + 1))),
        (j > 0, j < NY_DEV - 1,
         copy(start_ref.at[:, :, pl.ds(0, K // 2)], row_in.at[1], HALO + 3, at_y(j - 1))),
    ]
    for sends, _, move in halo:
        pl.when(sends)(move.start)

    ops_x = []
    for n, (ref, number) in enumerate(((fwd_x_ref, FX), (back_x_ref, BX))):
        ops_x.append([
            copy(ref, got_x.at[n, 0], number, at_x(xp[0])),
            copy(ref, got_x.at[n, 1], number + 1, at_x(xp[1])),
            copy(got_x.at[n, 1], got_x.at[n, 2], number + 2, at_x(xp[0])),
        ])
    ops_y = []
    for n, (ref, number) in enumerate(((fwd_y_ref, FY), (back_y_ref, BY))):
        ops_y.append([
            copy(ref, got_y.at[n, d], number + d, at_y(yp[d])) for d in range(3)
        ])
    fetches[0].wait()
    ops_x[0][1].start()
    ops_x[0][0].start()

    def widen(ref, target):
        high, low = split(ref[...])
        target[:, :K] = high
        target[:, K:] = low

    for move in fetches[1:] + cells[1:]:
        move.wait()
    widen(couple_x_ref, wide_c.at[0])
    widen(couple_y_ref, wide_c.at[1])
    widen(fwd_x_ref, wide_x.at[0, 0])
    widen(back_x_ref, wide_x.at[1, 0])
    widen(fwd_y_ref, wide_y.at[0, 0])
    widen(back_y_ref, wide_y.at[1, 0])

    permit = jnp.zeros((C, K), jnp.float32)
    for c in range(8):
        permit = jnp.where(classes_ref[...] == c, perm_ref[c], permit)
    permit_ref[...] = permit

    lane = lax.broadcasted_iota(jnp.int32, (C, K), 1)
    col = lax.broadcasted_iota(jnp.int32, (C, K), 0)
    node = lane % Z
    mine = lane // Z == col

    for n, target in ((0, edge_in.at[0]), (1, edge_in.at[1]), (2, row_in.at[0]), (3, row_in.at[1])):
        _, receives, move = halo[n]
        pl.when(receives)(move.wait_recv)

        def clear(target=target):
            target[...] = jnp.zeros(target.shape, jnp.float32)
        pl.when(jnp.logical_not(receives))(clear)

    def by_four(body):
        def four(q, _):
            for r in range(4):
                body(4 * q + r, 0)
            return 0

        lax.fori_loop(0, E // 4, four, 0)

    def residual(e, _):
        x = start_ref[e]
        low = edge_in[0, pl.ds(e, 1), :]
        high = edge_in[1, pl.ds(e, 1), :]
        after = jnp.where(col == C - 1, high, pltpu.roll(x, C - 1, 0))
        before = jnp.where(col == 0, low, pltpu.roll(x, 1, 0))
        piece = row_in[0, e]
        row_before = pltpu.roll(
            jnp.where(lane >= K - Z, jnp.concatenate([piece, piece], axis=1), x), Z, 1)
        piece = row_in[1, e]
        row_after = pltpu.roll(
            jnp.where(lane < Z, jnp.concatenate([piece, piece], axis=1), x), K - Z, 1)
        beside = after + before + row_after + row_before
        upper = jnp.where(node == Z - 1, 0.0, pltpu.roll(x, K - 1, 1))
        lower = jnp.where(node == 0, 0.0, pltpu.roll(x, 1, 1))
        source = jnp.where(conductor_ref[...] == e, drive_ref[...], 0.0)
        resid = source - (permit_ref[...] * (4.0 * x - beside) + 2.0 * x - (upper + lower))
        resid_ref[e] = resid
        src_ref[0, 0, pl.ds(e, 1), :] = jnp.sum(leaf_x_ref[...] * resid, axis=0, keepdims=True)
        return 0

    by_four(residual)

    def share(n, number, places):
        moves = [
            copy(src_ref.at[n, 0], src_ref.at[n, d + 1], number + d, places[d])
            for d in range(3)
        ]
        for move in reversed(moves):
            move.start()
        return moves

    def compose(n, wide, way, slot, order, position):
        def part(h, _):
            rows = pl.ds(pl.multiple_of(h * ROWS, ROWS), ROWS)

            def put(target, x):
                high, low = split(x * DOWN)
                target[n, rows, :K] = high
                target[n, rows, K:] = low

            pair = wide[way, slot(order[0]), rows, :]
            high, low = pair[:, :K], pair[:, K:]
            x = high.astype(jnp.float32) + low.astype(jnp.float32)
            pl.when(position == order[0])(functools.partial(put, prefix_ref, x))
            for k in order[1:]:
                x = product_of(high, low, wide[way, slot(k)])
                pl.when(position == k)(functools.partial(put, prefix_ref, x))
                high, low = split(x)
            put(whole_ref, x)
            whole_out[(3, 2, 0, 1)[n], rows, :] = x * DOWN
            return 0

        lax.fori_loop(0, K // ROWS, part, 0)

    def step_of(n, number, to):
        return copy(state_out.at[n], state_in.at[n], number, to)

    def inside(n, moves, wide, way, slot, order, position, first=None, step=None):
        for move in moves:
            move.wait_recv()
        state = src_ref[n, slot(order[0])] * DOWN
        kept = state
        for k in order[1:]:
            s = slot(k)
            state = product(state, wide[way, s]) + src_ref[n, s] * DOWN
            kept = jnp.where(position == k, state, kept)
        kept_ref[n] = kept
        if n == 1:
            tail_ref[n] = state

            def pass_tail():
                state_out[n] = state
                tail_x.start()
            pl.when(odd)(pass_tail)

            def clear():
                state_in[n] = jnp.zeros((E, K), jnp.float32)
            pl.when(gx >= 6)(clear)
            return
        if step is None:
            state_out[n] = state
            for a, _, move in tails[n - 2]:
                pl.when(rank[n - 2] == a)(move.start)
            return
        tail_ref[n] = state

        def begin():
            state_out[n] = state * UP
            step.start()
            state_in[n] = jnp.zeros((E, K), jnp.float32)
        pl.when(first)(begin)

        def pass_on():
            state_out[n] = state
            tail_f.start()
        pl.when((gx == 4) | (gx == 6))(pass_on)

    def entry_fwd_x():
        step = step_xf
        pl.when(((gx >= 1) & (gx <= 4)) | (gx == 6))(step.wait_recv)

        def pair():
            whole_f.wait_recv()
            widen(whole_in.at[3, 0], wide_f_in)
            tail_f.wait_recv()
            far_f.wait_recv()
            state_in[0] = (product(state_in[0], wide_f_in[...]) + tail_f_in[...]) * UP
        pl.when((gx == 5) | (gx == 7))(pair)

        def give():
            state_out[0] = (product(state_in[0], whole_ref[0]) + tail_ref[0]) * UP
            pl.when((gx == 3) | (gx == 5))(far_f.start)
            step.start()
        pl.when(((gx >= 1) & (gx <= 3)) | (gx == 5))(give)
        return (product(state_in[0], prefix_ref[0]) + kept_ref[0]) * UP

    def entry_y(n):
        state_in[n] = jnp.zeros((E, K), jnp.float32)
        for place in range(3):
            def take(place=place):
                for a, b, move in tails[n - 2]:
                    if a == place:
                        pl.when(rank[n - 2] == b)(move.wait_recv)
                state = tails_in[n - 2, place]
                if place:
                    state = product(state_in[n], wide_in[n - 2, place - 1]) + state
                state_in[n] = state * UP
            pl.when(rank[n - 2] > place)(take)
        return (product(state_in[n], prefix_ref[n]) + kept_ref[n]) * UP

    rank = (gy, G - 1 - gy)

    def member(way, place):
        return at_y((place if way == 0 else G - 1 - place) * G + jy)

    wholes = [
        [(a, b, copy(whole_out.at[n], whole_in.at[n, a - 1], WY + 3 * n + q, member(n, b)))
         for q, (a, b) in enumerate(WHOLE_PAIRS)]
        for n in range(2)
    ]
    tails = [
        [(a, b, copy(state_out.at[2 + n], tails_in.at[n, a], TY + 6 * n + q, member(n, b)))
         for q, (a, b) in enumerate(TAIL_PAIRS)]
        for n in range(2)
    ]
    up, down = (0, 1, 2, 3), (3, 2, 1, 0)
    x_first = i < G
    step_xf = step_of(0, EXF, at_x(i + G))
    far_f = step_of(0, EXF_FAR, at_x(i + 2 * G))
    tail_f = copy(state_out.at[0], tail_f_in, TXF, at_x(i + G))
    whole_f = copy(whole_out.at[3], whole_in.at[3, 0], WXF, at_x(i + G))
    odd = gx % 2 == 1
    even = jnp.logical_not(odd)
    far = step_of(1, EXB, at_x(i - 2 * G))
    near = step_of(1, EXB_NEAR, at_x(i - G))
    tail_x = copy(state_out.at[1], tail_x_in, TX, at_x(i - G))
    whole_x = copy(whole_out.at[2], whole_in.at[2, 0], WX, at_x(i - G))

    def entry_back_x():
        pl.when(odd & (gx < 6))(near.wait_recv)

        def pair():
            pl.when(gx < 6)(far.wait_recv)
            tail_x.wait_recv()

            def through():
                state_in[1] = (product(state_in[1], wide_x_in[...]) + tail_x_in[...]) * UP
            pl.when(gx < 6)(through)

            def only():
                state_in[1] = tail_x_in[...] * UP
            pl.when(gx >= 6)(only)

            def give():
                state_out[1] = (product(state_in[1], whole_ref[1]) + tail_ref[1]) * UP
                far.start()
                near.start()
            pl.when(gx >= 2)(give)
        pl.when(even)(pair)
        return (product(state_in[1], prefix_ref[1]) + kept_ref[1]) * UP

    early = i < NX_DEV // 2
    late = jnp.logical_not(early)
    before = i < NX_DEV - 2 * G

    def receive_x(n):
        ops_x[n][1].wait_recv()
        ops_x[n][2].start()
        widen(got_x.at[n, 1], wide_x.at[n, 2])
        ops_x[n][0].wait_recv()
        widen(got_x.at[n, 0], wide_x.at[n, 1])
        ops_x[n][2].wait_recv()
        widen(got_x.at[n, 2], wide_x.at[n, 3])

    def ready_back_x():
        receive_x(1)
        compose(1, wide_x, 1, slot_x, down, ix)
        pl.when(odd & (gx < 6))(whole_x.start)

    def ready_y():
        for n, order in ((0, up), (1, down)):
            for d in range(3):
                ops_y[n][d].wait_recv()
                widen(got_y.at[n, d], wide_y.at[n, d + 1])
            compose(2 + n, wide_y, n, slot_y, order, jy)
            for a, _, move in wholes[n]:
                pl.when(rank[n] == a)(move.start)
        for n in range(2):
            for a, b, move in wholes[n]:
                def take(a=a, move=move, n=n):
                    move.wait_recv()
                    widen(whole_in.at[n, a - 1], wide_in.at[n, a - 1])
                pl.when(rank[n] == b)(take)

    moves_sx = share(0, SX, [at_x(p) for p in xp])
    receive_x(0)
    inside(0, moves_sx, wide_x, 0, slot_x, up, ix, x_first, step_xf)
    ops_x[1][1].start()
    ops_x[1][0].start()
    for n in range(2):
        for move in ops_y[n]:
            move.start()
    compose(0, wide_x, 0, slot_x, up, ix)
    pl.when((gx == 4) | (gx == 6))(whole_f.start)
    pl.when(late)(ready_back_x)
    ahead = entry_fwd_x()
    src_ref[1, 0] = product(ahead, wide_c[0])
    moves_qx = share(1, QX, [at_x(p) for p in xp])
    pl.when(early)(ready_back_x)
    inside(1, moves_qx, wide_x, 1, slot_x, down, ix)

    def take_whole_x():
        whole_x.wait_recv()
        widen(whole_in.at[2, 0], wide_x_in)
    pl.when(even & (gx < 6))(take_whole_x)
    pl.when(before)(ready_y)
    across_ref[...] = entry_back_x()

    def gather_y(e, _):
        lifted = resid_ref[e] + leaf_x_ref[...] * across_ref[pl.ds(e, 1), :]
        t = lifted * leaf_y_ref[...]
        for shift in (128, 64, 32, 16):
            t = t + pltpu.roll(t, shift, 1)
        src_ref[2, 0, pl.ds(e, 1), :] = jnp.sum(jnp.where(mine, t, 0.0), axis=0, keepdims=True)
        return 0

    by_four(gather_y)
    moves_sy = share(2, SY, [at_y(p) for p in yp])
    pl.when(jnp.logical_not(before))(ready_y)
    inside(2, moves_sy, wide_y, 0, slot_y, up, jy)
    ahead = entry_y(2)
    src_ref[3, 0] = product(ahead, wide_c[1])
    moves_qy = share(3, QY, [at_y(p) for p in yp])
    inside(3, moves_qy, wide_y, 1, slot_y, down, jy)
    along_ref[...] = entry_y(3)

    def finish(e, _):
        t = jnp.where(mine, along_ref[pl.ds(e, 1), :], 0.0)
        for shift in (128, 64, 32, 16):
            t = t + pltpu.roll(t, shift, 1)
        out_ref[e] = (
            start_ref[e] + leaf_x_ref[...] * across_ref[pl.ds(e, 1), :] + leaf_y_ref[...] * t
        )
        return 0

    by_four(finish)

    for sends, _, move in halo:
        pl.when(sends)(move.wait_send)
    for moves in ops_x + ops_y + [moves_sx, moves_qx, moves_sy, moves_qy]:
        for move in moves:
            move.wait_send()
    pl.when((gx <= 3) | (gx == 5))(step_xf.wait_send)
    pl.when((gx == 3) | (gx == 5))(far_f.wait_send)
    for move in (tail_f, whole_f):
        pl.when((gx == 4) | (gx == 6))(move.wait_send)
    for move in (far, near):
        pl.when(even & (gx >= 2))(move.wait_send)
    pl.when(odd)(tail_x.wait_send)
    pl.when(odd & (gx < 6))(whole_x.wait_send)
    for n in range(2):
        for a, _, move in wholes[n] + tails[n]:
            pl.when(rank[n] == a)(move.wait_send)


def local(*arrays):
    vmem = pl.BlockSpec(memory_space=pltpu.VMEM)
    smem = pl.BlockSpec(memory_space=pltpu.SMEM)
    hbm = pl.BlockSpec(memory_space=pl.ANY)
    f32, bf16 = jnp.float32, jnp.bfloat16
    return pl.pallas_call(
        kernel,
        out_shape=jax.ShapeDtypeStruct((E, C, K), f32),
        in_specs=[hbm] * 4 + [smem] + [hbm] * 8,
        out_specs=vmem,
        scratch_shapes=[
            pltpu.VMEM((6, K, K), f32),
            pltpu.VMEM((E, K), f32),
            pltpu.VMEM((K, 2 * K), bf16),
            pltpu.VMEM((E, K), f32),
            pltpu.VMEM((K, 2 * K), bf16),
            pltpu.VMEM((E, C, K), f32),
            pltpu.VMEM((C, K), jnp.int32),
            pltpu.VMEM((C, K), jnp.int32),
            pltpu.VMEM((C, K), f32),
            pltpu.VMEM((C, K), f32),
            pltpu.VMEM((C, K), f32),
            pltpu.VMEM((2, E, K), f32),
            pltpu.VMEM((2, E, K), f32),
            pltpu.VMEM((2, E, C, K // 2), f32),
            pltpu.VMEM((E, C, K), f32),
            pltpu.VMEM((C, K), f32),
            pltpu.VMEM((2, 3, K, K), f32),
            pltpu.VMEM((2, 3, K, K), f32),
            pltpu.VMEM((2, G, K, 2 * K), bf16),
            pltpu.VMEM((2, G, K, 2 * K), bf16),
            pltpu.VMEM((2, K, 2 * K), bf16),
            pltpu.VMEM((4, K, 2 * K), bf16),
            pltpu.VMEM((4, K, 2 * K), bf16),
            pltpu.VMEM((4, K, K), f32),
            pltpu.VMEM((4, 2, K, K), f32),
            pltpu.VMEM((2, 2, K, 2 * K), bf16),
            pltpu.VMEM((4, G, E, K), f32),
            pltpu.VMEM((4, E, K), f32),
            pltpu.VMEM((4, E, K), f32),
            pltpu.VMEM((4, E, K), f32),
            pltpu.VMEM((4, E, K), f32),
            pltpu.VMEM((2, 3, E, K), f32),
            pltpu.VMEM((E, K), f32),
            pltpu.VMEM((E, K), f32),
            pltpu.SemaphoreType.DMA((COPIES,)),
            pltpu.SemaphoreType.DMA((COPIES,)),
            pltpu.SemaphoreType.DMA((12,)),
        ],
        compiler_params=pltpu.CompilerParams(
            collective_id=0, has_side_effects=True, vmem_limit_bytes=63 * 1024 * 1024
        ),
    )(*arrays)


def solution(mesh):
    split_two = P("gx", "gy")
    in_specs = (P(None, "gx", "gy"),) + (split_two,) * 3 + (P(),) + (split_two,) * 8
    return jax.shard_map(
        local, mesh=mesh, in_specs=in_specs, out_specs=P(None, "gx", "gy"), check_vma=False
    )
```

```python
import functools

import jax
import jax.numpy as jnp
from jax import lax
from jax.experimental import pallas as pl
from jax.experimental.pallas import tpu as pltpu
from jax.sharding import PartitionSpec as P

Z = 16
E = 16
C = 16
K = 256
NX_DEV = 32
NY_DEV = 16
G = 4
MESH = pl.DeviceIdType.MESH

HALO = 0
FX, BX, FY, BY = 4, 7, 10, 13
SX, QX, SY, QY = 16, 19, 22, 25
EXF, EXB = 28, 29
WY = 30
TY = 36
EXB_NEAR, TX, WX = 48, 49, 50
COPIES = 51
WHOLE_PAIRS = ((1, 2), (1, 3), (2, 3))
TAIL_PAIRS = ((0, 1), (0, 2), (0, 3), (1, 2), (1, 3), (2, 3))

DOWN, UP = 2.0**-24, 2.0**24
ROWS = 128


def split(x):
    high = x.astype(jnp.bfloat16)
    low = (x - high.astype(jnp.float32)).astype(jnp.bfloat16)
    return high, low


def product_of(high, low, wide):
    rows = high.shape[0]
    r = jnp.dot(
        jnp.concatenate([high, low], axis=0), wide, preferred_element_type=jnp.float32
    )
    return (r[rows:, K:] + r[:rows, K:] + r[rows:, :K]) + r[:rows, :K]


def product(state, wide):
    return product_of(*split(state), wide)


def kernel(
    start_hbm, classes_hbm, conductor_hbm, drive_hbm, perm_ref, leaf_x_hbm, leaf_y_hbm,
    fwd_x_hbm, back_x_hbm, couple_x_hbm, fwd_y_hbm, back_y_hbm, couple_y_hbm,
    out_ref,
    own_ref, tail_x_in, wide_x_in,
    start_ref, classes_ref, conductor_ref, drive_ref, leaf_x_ref, leaf_y_ref,
    edge_out, edge_in, row_in, resid_ref, permit_ref,
    got_x, got_y, wide_x, wide_y, wide_c, whole_ref, prefix_ref, whole_out, whole_in, wide_in,
    src_ref, kept_ref, tail_ref, state_out, state_in, tails_in, across_ref, along_ref,
    send_sem, recv_sem, own_sem,
):
    fetches = [
        pltpu.make_async_copy(ref, own_ref.at[n], own_sem.at[n])
        for n, ref in enumerate(
            (fwd_x_hbm, couple_x_hbm, couple_y_hbm, back_x_hbm, fwd_y_hbm, back_y_hbm))
    ]
    cells = [
        pltpu.make_async_copy(src, dst, own_sem.at[6 + n])
        for n, (src, dst) in enumerate((
            (start_hbm, start_ref), (classes_hbm, classes_ref), (conductor_hbm, conductor_ref),
            (drive_hbm, drive_ref), (leaf_x_hbm, leaf_x_ref), (leaf_y_hbm, leaf_y_ref)))
    ]
    fwd_x_ref, couple_x_ref, couple_y_ref, back_x_ref, fwd_y_ref, back_y_ref = (
        own_ref.at[n] for n in range(6))
    i = lax.axis_index("gx")
    j = lax.axis_index("gy")
    ix, gx = i % G, i // G
    jy, gy = j % G, j // G
    core, chip = ix % 2, ix // 2

    def at_x(index):
        return (index, j)

    def at_y(index):
        return (i, index)

    xp = [
        gx * G + 2 * chip + (1 - core),
        gx * G + 2 * (1 - chip) + core,
        gx * G + 2 * (1 - chip) + (1 - core),
    ]
    yp = [gy * G + (jy + d) % G for d in (1, 2, 3)]

    def slot_x(k):
        return 2 * ((chip + k // 2) % 2) + (core + k % 2) % 2

    def slot_y(k):
        return (jy + G - k) % G

    partners = [(None, at_x(p)) for p in xp] + [(None, at_y(p)) for p in yp]
    partners += [(None, at_y((gy + q) % G * G + jy)) for q in (1, 2, 3)]
    partners += [
        ((ix == 0) & (i > 0), at_x(i - 1)),
        ((ix == G - 1) & (i < NX_DEV - 1), at_x(i + 1)),
        (i >= G, at_x(i - G)),
        (i < NX_DEV - G, at_x(i + G)),
        ((gx % 2 == 0) & (gx >= 2), at_x(i - 2 * G)),
        ((gx % 2 == 0) & (gx <= 4), at_x(i + 2 * G)),
        ((jy == 0) & (j > 0), at_y(j - 1)),
        ((jy == G - 1) & (j < NY_DEV - 1), at_y(j + 1)),
    ]
    barrier = pltpu.get_barrier_semaphore()
    for held, where in partners:
        def greet(where=where):
            pl.semaphore_signal(barrier, inc=1, device_id=where, device_id_type=MESH)
        if held is None:
            greet()
        else:
            pl.when(held)(greet)
    for move in cells[:1] + fetches[:1] + cells[1:] + fetches[1:]:
        move.start()
    cells[0].wait()
    edge_out[0] = start_ref[:, C - 1, :]
    edge_out[1] = start_ref[:, 0, :]
    count = 9
    for held, _ in partners[9:]:
        count = count + held.astype(jnp.int32)
    pl.semaphore_wait(barrier, count)

    def copy(src, dst, number, where):
        return pltpu.make_async_remote_copy(
            src_ref=src, dst_ref=dst, send_sem=send_sem.at[number],
            recv_sem=recv_sem.at[number], device_id=where, device_id_type=MESH,
        )

    halo = [
        (i < NX_DEV - 1, i > 0, copy(edge_out.at[0], edge_in.at[0], HALO, at_x(i + 1))),
        (i > 0, i < NX_DEV - 1, copy(edge_out.at[1], edge_in.at[1], HALO + 1, at_x(i - 1))),
        (j < NY_DEV - 1, j > 0,
         copy(start_ref.at[:, :, pl.ds(K // 2, K // 2)], row_in.at[0], HALO + 2, at_y(j + 1))),
        (j > 0, j < NY_DEV - 1,
         copy(start_ref.at[:, :, pl.ds(0, K // 2)], row_in.at[1], HALO + 3, at_y(j - 1))),
    ]
    for sends, _, move in halo:
        pl.when(sends)(move.start)

    ops_x = []
    for n, (ref, number) in enumerate(((fwd_x_ref, FX), (back_x_ref, BX))):
        ops_x.append([
            copy(ref, got_x.at[n, 0], number, at_x(xp[0])),
            copy(ref, got_x.at[n, 1], number + 1, at_x(xp[1])),
            copy(got_x.at[n, 1], got_x.at[n, 2], number + 2, at_x(xp[0])),
        ])
    ops_y = []
    for n, (ref, number) in enumerate(((fwd_y_ref, FY), (back_y_ref, BY))):
        ops_y.append([
            copy(ref, got_y.at[n, d], number + d, at_y(yp[d])) for d in range(3)
        ])
    fetches[0].wait()
    ops_x[0][1].start()
    ops_x[0][0].start()

    def widen(ref, target):
        high, low = split(ref[...])
        target[:, :K] = high
        target[:, K:] = low

    for move in fetches[1:] + cells[1:]:
        move.wait()
    widen(couple_x_ref, wide_c.at[0])
    widen(couple_y_ref, wide_c.at[1])
    widen(fwd_x_ref, wide_x.at[0, 0])
    widen(back_x_ref, wide_x.at[1, 0])
    widen(fwd_y_ref, wide_y.at[0, 0])
    widen(back_y_ref, wide_y.at[1, 0])

    permit = jnp.zeros((C, K), jnp.float32)
    for c in range(8):
        permit = jnp.where(classes_ref[...] == c, perm_ref[c], permit)
    permit_ref[...] = permit

    lane = lax.broadcasted_iota(jnp.int32, (C, K), 1)
    col = lax.broadcasted_iota(jnp.int32, (C, K), 0)
    node = lane % Z
    mine = lane // Z == col

    for n, target in ((0, edge_in.at[0]), (1, edge_in.at[1]), (2, row_in.at[0]), (3, row_in.at[1])):
        _, receives, move = halo[n]
        pl.when(receives)(move.wait_recv)

        def clear(target=target):
            target[...] = jnp.zeros(target.shape, jnp.float32)
        pl.when(jnp.logical_not(receives))(clear)

    def by_four(body):
        def four(q, _):
            for r in range(4):
                body(4 * q + r, 0)
            return 0

        lax.fori_loop(0, E // 4, four, 0)

    def residual(e, _):
        x = start_ref[e]
        low = edge_in[0, pl.ds(e, 1), :]
        high = edge_in[1, pl.ds(e, 1), :]
        after = jnp.where(col == C - 1, high, pltpu.roll(x, C - 1, 0))
        before = jnp.where(col == 0, low, pltpu.roll(x, 1, 0))
        piece = row_in[0, e]
        row_before = pltpu.roll(
            jnp.where(lane >= K - Z, jnp.concatenate([piece, piece], axis=1), x), Z, 1)
        piece = row_in[1, e]
        row_after = pltpu.roll(
            jnp.where(lane < Z, jnp.concatenate([piece, piece], axis=1), x), K - Z, 1)
        beside = after + before + row_after + row_before
        upper = jnp.where(node == Z - 1, 0.0, pltpu.roll(x, K - 1, 1))
        lower = jnp.where(node == 0, 0.0, pltpu.roll(x, 1, 1))
        source = jnp.where(conductor_ref[...] == e, drive_ref[...], 0.0)
        resid = source - (permit_ref[...] * (4.0 * x - beside) + 2.0 * x - (upper + lower))
        resid_ref[e] = resid
        src_ref[0, 0, pl.ds(e, 1), :] = jnp.sum(leaf_x_ref[...] * resid, axis=0, keepdims=True)
        return 0

    by_four(residual)

    def share(n, number, places):
        moves = [
            copy(src_ref.at[n, 0], src_ref.at[n, d + 1], number + d, places[d])
            for d in range(3)
        ]
        for move in reversed(moves):
            move.start()
        return moves

    def compose(n, wide, way, slot, order, position):
        def part(h, _):
            rows = pl.ds(pl.multiple_of(h * ROWS, ROWS), ROWS)

            def put(target, x):
                high, low = split(x * DOWN)
                target[n, rows, :K] = high
                target[n, rows, K:] = low

            pair = wide[way, slot(order[0]), rows, :]
            high, low = pair[:, :K], pair[:, K:]
            x = high.astype(jnp.float32) + low.astype(jnp.float32)
            pl.when(position == order[0])(functools.partial(put, prefix_ref, x))
            for k in order[1:]:
                x = product_of(high, low, wide[way, slot(k)])
                pl.when(position == k)(functools.partial(put, prefix_ref, x))
                high, low = split(x)
            put(whole_ref, x)
            if n >= 1:
                whole_out[(n + 1) % 3, rows, :] = x * DOWN
            return 0

        lax.fori_loop(0, K // ROWS, part, 0)

    def step_of(n, number, to):
        return copy(state_out.at[n], state_in.at[n], number, to)

    def inside(n, moves, wide, way, slot, order, position, first=None, step=None):
        for move in moves:
            move.wait_recv()
        state = src_ref[n, slot(order[0])] * DOWN
        kept = state
        for k in order[1:]:
            s = slot(k)
            state = product(state, wide[way, s]) + src_ref[n, s] * DOWN
            kept = jnp.where(position == k, state, kept)
        kept_ref[n] = kept
        if n == 1:
            tail_ref[n] = state

            def pass_tail():
                state_out[n] = state
                tail_x.start()
            pl.when(odd)(pass_tail)

            def clear():
                state_in[n] = jnp.zeros((E, K), jnp.float32)
            pl.when(gx >= 6)(clear)
            return
        if step is None:
            state_out[n] = state
            for a, _, move in tails[n - 2]:
                pl.when(rank[n - 2] == a)(move.start)
            return
        tail_ref[n] = state

        def begin():
            state_out[n] = state * UP
            step.start()
            state_in[n] = jnp.zeros((E, K), jnp.float32)
        pl.when(first)(begin)

    def across_groups(n, first, last, step):
        def take():
            step.wait_recv()
        pl.when(jnp.logical_not(first))(take)

        def give():
            state_out[n] = (product(state_in[n], whole_ref[n]) + tail_ref[n]) * UP
            step.start()
        pl.when(jnp.logical_not(first) & jnp.logical_not(last))(give)
        return (product(state_in[n], prefix_ref[n]) + kept_ref[n]) * UP

    def entry_y(n):
        state_in[n] = jnp.zeros((E, K), jnp.float32)
        for place in range(3):
            def take(place=place):
                for a, b, move in tails[n - 2]:
                    if a == place:
                        pl.when(rank[n - 2] == b)(move.wait_recv)
                state = tails_in[n - 2, place]
                if place:
                    state = product(state_in[n], wide_in[n - 2, place - 1]) + state
                state_in[n] = state * UP
            pl.when(rank[n - 2] > place)(take)
        return (product(state_in[n], prefix_ref[n]) + kept_ref[n]) * UP

    rank = (gy, G - 1 - gy)

    def member(way, place):
        return at_y((place if way == 0 else G - 1 - place) * G + jy)

    wholes = [
        [(a, b, copy(whole_out.at[n], whole_in.at[n, a - 1], WY + 3 * n + q, member(n, b)))
         for q, (a, b) in enumerate(WHOLE_PAIRS)]
        for n in range(2)
    ]
    tails = [
        [(a, b, copy(state_out.at[2 + n], tails_in.at[n, a], TY + 6 * n + q, member(n, b)))
         for q, (a, b) in enumerate(TAIL_PAIRS)]
        for n in range(2)
    ]
    up, down = (0, 1, 2, 3), (3, 2, 1, 0)
    x_first, x_last = i < G, i >= NX_DEV - G
    step_xf = step_of(0, EXF, at_x(i + G))
    odd = gx % 2 == 1
    even = jnp.logical_not(odd)
    far = step_of(1, EXB, at_x(i - 2 * G))
    near = step_of(1, EXB_NEAR, at_x(i - G))
    tail_x = copy(state_out.at[1], tail_x_in, TX, at_x(i - G))
    whole_x = copy(whole_out.at[2], whole_in.at[2, 0], WX, at_x(i - G))

    def entry_back_x():
        pl.when(odd & (gx < 6))(near.wait_recv)

        def pair():
            pl.when(gx < 6)(far.wait_recv)
            tail_x.wait_recv()

            def through():
                state_in[1] = (product(state_in[1], wide_x_in[...]) + tail_x_in[...]) * UP
            pl.when(gx < 6)(through)

            def only():
                state_in[1] = tail_x_in[...] * UP
            pl.when(gx >= 6)(only)

            def give():
                state_out[1] = (product(state_in[1], whole_ref[1]) + tail_ref[1]) * UP
                far.start()
                near.start()
            pl.when(gx >= 2)(give)
        pl.when(even)(pair)
        return (product(state_in[1], prefix_ref[1]) + kept_ref[1]) * UP

    early = i < NX_DEV // 2
    late = jnp.logical_not(early)
    before = i < NX_DEV - 2 * G

    def receive_x(n):
        ops_x[n][1].wait_recv()
        ops_x[n][2].start()
        widen(got_x.at[n, 1], wide_x.at[n, 2])
        ops_x[n][0].wait_recv()
        widen(got_x.at[n, 0], wide_x.at[n, 1])
        ops_x[n][2].wait_recv()
        widen(got_x.at[n, 2], wide_x.at[n, 3])

    def ready_back_x():
        receive_x(1)
        compose(1, wide_x, 1, slot_x, down, ix)
        pl.when(odd & (gx < 6))(whole_x.start)

    def ready_y():
        for n, order in ((0, up), (1, down)):
            for d in range(3):
                ops_y[n][d].wait_recv()
                widen(got_y.at[n, d], wide_y.at[n, d + 1])
            compose(2 + n, wide_y, n, slot_y, order, jy)
            for a, _, move in wholes[n]:
                pl.when(rank[n] == a)(move.start)
        for n in range(2):
            for a, b, move in wholes[n]:
                def take(a=a, move=move, n=n):
                    move.wait_recv()
                    widen(whole_in.at[n, a - 1], wide_in.at[n, a - 1])
                pl.when(rank[n] == b)(take)

    moves_sx = share(0, SX, [at_x(p) for p in xp])
    receive_x(0)
    inside(0, moves_sx, wide_x, 0, slot_x, up, ix, x_first, step_xf)
    ops_x[1][1].start()
    ops_x[1][0].start()
    for n in range(2):
        for move in ops_y[n]:
            move.start()
    compose(0, wide_x, 0, slot_x, up, ix)
    pl.when(late)(ready_back_x)
    ahead = across_groups(0, x_first, x_last, step_xf)
    src_ref[1, 0] = product(ahead, wide_c[0])
    moves_qx = share(1, QX, [at_x(p) for p in xp])
    pl.when(early)(ready_back_x)
    inside(1, moves_qx, wide_x, 1, slot_x, down, ix)

    def take_whole_x():
        whole_x.wait_recv()
        widen(whole_in.at[2, 0], wide_x_in)
    pl.when(even & (gx < 6))(take_whole_x)
    pl.when(before)(ready_y)
    across_ref[...] = entry_back_x()

    def gather_y(e, _):
        lifted = resid_ref[e] + leaf_x_ref[...] * across_ref[pl.ds(e, 1), :]
        t = lifted * leaf_y_ref[...]
        for shift in (128, 64, 32, 16):
            t = t + pltpu.roll(t, shift, 1)
        src_ref[2, 0, pl.ds(e, 1), :] = jnp.sum(jnp.where(mine, t, 0.0), axis=0, keepdims=True)
        return 0

    by_four(gather_y)
    moves_sy = share(2, SY, [at_y(p) for p in yp])
    pl.when(jnp.logical_not(before))(ready_y)
    inside(2, moves_sy, wide_y, 0, slot_y, up, jy)
    ahead = entry_y(2)
    src_ref[3, 0] = product(ahead, wide_c[1])
    moves_qy = share(3, QY, [at_y(p) for p in yp])
    inside(3, moves_qy, wide_y, 1, slot_y, down, jy)
    along_ref[...] = entry_y(3)

    def finish(e, _):
        t = jnp.where(mine, along_ref[pl.ds(e, 1), :], 0.0)
        for shift in (128, 64, 32, 16):
            t = t + pltpu.roll(t, shift, 1)
        out_ref[e] = (
            start_ref[e] + leaf_x_ref[...] * across_ref[pl.ds(e, 1), :] + leaf_y_ref[...] * t
        )
        return 0

    by_four(finish)

    for sends, _, move in halo:
        pl.when(sends)(move.wait_send)
    for moves in ops_x + ops_y + [moves_sx, moves_qx, moves_sy, moves_qy]:
        for move in moves:
            move.wait_send()
    pl.when(jnp.logical_not(x_last))(step_xf.wait_send)
    for move in (far, near):
        pl.when(even & (gx >= 2))(move.wait_send)
    pl.when(odd)(tail_x.wait_send)
    pl.when(odd & (gx < 6))(whole_x.wait_send)
    for n in range(2):
        for a, _, move in wholes[n] + tails[n]:
            pl.when(rank[n] == a)(move.wait_send)


def local(*arrays):
    vmem = pl.BlockSpec(memory_space=pltpu.VMEM)
    smem = pl.BlockSpec(memory_space=pltpu.SMEM)
    hbm = pl.BlockSpec(memory_space=pl.ANY)
    f32, bf16 = jnp.float32, jnp.bfloat16
    return pl.pallas_call(
        kernel,
        out_shape=jax.ShapeDtypeStruct((E, C, K), f32),
        in_specs=[hbm] * 4 + [smem] + [hbm] * 8,
        out_specs=vmem,
        scratch_shapes=[
            pltpu.VMEM((6, K, K), f32),
            pltpu.VMEM((E, K), f32),
            pltpu.VMEM((K, 2 * K), bf16),
            pltpu.VMEM((E, C, K), f32),
            pltpu.VMEM((C, K), jnp.int32),
            pltpu.VMEM((C, K), jnp.int32),
            pltpu.VMEM((C, K), f32),
            pltpu.VMEM((C, K), f32),
            pltpu.VMEM((C, K), f32),
            pltpu.VMEM((2, E, K), f32),
            pltpu.VMEM((2, E, K), f32),
            pltpu.VMEM((2, E, C, K // 2), f32),
            pltpu.VMEM((E, C, K), f32),
            pltpu.VMEM((C, K), f32),
            pltpu.VMEM((2, 3, K, K), f32),
            pltpu.VMEM((2, 3, K, K), f32),
            pltpu.VMEM((2, G, K, 2 * K), bf16),
            pltpu.VMEM((2, G, K, 2 * K), bf16),
            pltpu.VMEM((2, K, 2 * K), bf16),
            pltpu.VMEM((4, K, 2 * K), bf16),
            pltpu.VMEM((4, K, 2 * K), bf16),
            pltpu.VMEM((3, K, K), f32),
            pltpu.VMEM((3, 2, K, K), f32),
            pltpu.VMEM((2, 2, K, 2 * K), bf16),
            pltpu.VMEM((4, G, E, K), f32),
            pltpu.VMEM((4, E, K), f32),
            pltpu.VMEM((4, E, K), f32),
            pltpu.VMEM((4, E, K), f32),
            pltpu.VMEM((4, E, K), f32),
            pltpu.VMEM((2, 3, E, K), f32),
            pltpu.VMEM((E, K), f32),
            pltpu.VMEM((E, K), f32),
            pltpu.SemaphoreType.DMA((COPIES,)),
            pltpu.SemaphoreType.DMA((COPIES,)),
            pltpu.SemaphoreType.DMA((12,)),
        ],
        compiler_params=pltpu.CompilerParams(
            collective_id=0, has_side_effects=True, vmem_limit_bytes=63 * 1024 * 1024
        ),
    )(*arrays)


def solution(mesh):
    split_two = P("gx", "gy")
    in_specs = (P(None, "gx", "gy"),) + (split_two,) * 3 + (P(),) + (split_two,) * 8
    return jax.shard_map(
        local, mesh=mesh, in_specs=in_specs, out_specs=P(None, "gx", "gy"), check_vma=False
    )
```
